256 devices in a mesh: seq: 32 (over y_lo, z, core), tp: 8 (over x, y_hi).
Axes of the slice: x: 4, y: 4 (y_hi: 2, y_lo: 2; y = y_hi * 2 + y_lo), z: 8, core: 2. Of those that a mesh axis runs over, the one named last changes fastest.
Arguments:
- query: bfloat16 [6144, 5120], P('seq', 'tp')
- span_keys: bfloat16 [6144, 5120], P('seq', 'tp'), may hold values from -6 to 6
- span_values: bfloat16 [6144, 5120], P('seq', 'tp'), may hold values from -48 to 48
- cache_keys: bfloat16 [8, 8192, 5120], P(None, 'seq', 'tp'), may hold values from -6 to 6
- cache_values: bfloat16 [8, 8192, 5120], P(None, 'seq', 'tp'), may hold values from -48 to 48
- out_weight: bfloat16 [5120, 5120], P('tp'), may hold values from -0.078125 to 0.078125
- cache_lengths: int32 [8], replicated, may hold values from 1 to 8192, as said below
- sink_counts: int32 [8], replicated, may hold values from 1 to 256, as said below
- windows: int32 [8], replicated, may hold values from 2048 to 4096, as said below
- block_of_slot: int32 [8, 32], replicated, may hold values from 0 to 31, each once within a row
Outputs:
- projected: bfloat16 [6144, 5120], P('seq', 'tp')
The draws below stay inside these ranges and needn't reach their ends.
Inputs may be any that keep to these rules, and one draw needn't show every extreme that they name: `cache_lengths`: at least 1 and at most 8192; some request has exactly 8192. `sink_counts`: some request has exactly 256. `windows`: some request has exactly 4096. `block_of_slot`: each row is a permutation of 0 to 31.
All inputs are finite; a program needn't handle non-finite values.
Results may differ from the reference program's by a relative error of at most 0.015.
Values may be sent and summed in bfloat16 or wider, within the bound.
A program may use at most 192 MiB of HBM per device.

```python
import math
import jax
import jax.numpy as jnp
from jax import lax

HEADS = 40
HEAD = 128
D = 5120
Q_DEV = 192
CACHE_DEV = 256
GROUP = 4
SPAN = 768
REQUESTS = 8
TOKENS = 6144
CACHE_MAX = 8192
WINDOW = 4096
SINK_MAX = 256
N_SEQ = 32


def draw_query(key, part):
    base = jax.random.normal(key, (TOKENS, D), jnp.float32)
    return jnp.clip(base, -60.0, 60.0).astype(jnp.bfloat16)


def draw_cache_lengths(key, part):
    first, second, third = jax.random.split(jax.random.fold_in(key, 11), 3)
    shifts = jax.random.randint(first, (REQUESTS,), 0, 6)
    tops = jnp.right_shift(jnp.full((REQUESTS,), CACHE_MAX, jnp.int32), shifts)
    cuts = jax.random.randint(second, (REQUESTS,), 0, tops // 2 + 1)
    lengths = tops - cuts
    chosen = jax.random.randint(third, (), 0, REQUESTS)
    return jnp.where(jnp.arange(REQUESTS) == chosen, CACHE_MAX, lengths).astype(jnp.int32)


def draw_sink_counts(key, part):
    first, second = jax.random.split(jax.random.fold_in(key, 13))
    counts = jax.random.randint(first, (REQUESTS,), 1, SINK_MAX + 1)
    chosen = jax.random.randint(second, (), 0, REQUESTS)
    return jnp.where(jnp.arange(REQUESTS) == chosen, SINK_MAX, counts).astype(jnp.int32)


def draw_windows(key, part):
    first, second = jax.random.split(jax.random.fold_in(key, 17))
    sizes = jax.random.randint(first, (REQUESTS,), WINDOW // 2, WINDOW + 1)
    chosen = jax.random.randint(second, (), 0, REQUESTS)
    return jnp.where(jnp.arange(REQUESTS) == chosen, WINDOW, sizes).astype(jnp.int32)


def block_levels(stream_key, extent, cuts, smallest, top_value):
    loudness, own = 1.0, jax.random.fold_in(stream_key, 6)
    for dim, shards_of in cuts:
        steps = jnp.exp(jax.random.uniform(jax.random.fold_in(own, dim), (shards_of,), jnp.float32, smallest / len(cuts), top_value / len(cuts)))
        loudness = loudness * jnp.repeat(steps, extent[dim] // shards_of).reshape([-1 if axis == dim else 1 for axis in range(len(extent))])
    return loudness


def noise(rng, shape, spread, bound, cuts=(), kind=jnp.bfloat16):
    gain = block_levels(rng, shape, cuts, -0.22, 0.18) if cuts else 1.0
    result = jax.random.normal(rng, shape, jnp.float32) * spread * gain
    return jnp.minimum(jnp.maximum(result, -bound), bound).astype(kind)


def setup_inputs(seed: int = 0) -> dict:
    key_list = jax.random.split(jax.random.key(seed), 11)
    query = draw_query(jax.random.fold_in(key_list[10], 71), 0)
    span_keys = noise(key_list[1], (TOKENS, D), 1.0, 6.0, ((0, 32), (1, 8)))
    span_values = noise(key_list[2], (TOKENS, D), 8.0, 48.0, ((0, 32), (1, 8)))
    cache_keys = noise(key_list[3], (REQUESTS, CACHE_MAX, D), 1.0, 6.0, ((1, 32), (2, 8)))
    cache_values = noise(key_list[4], (REQUESTS, CACHE_MAX, D), 8.0, 48.0, ((1, 32), (2, 8)))
    out_weight = noise(key_list[5], (D, D), D ** -0.5, 0.078125, ((0, 8),))
    cache_lengths = draw_cache_lengths(jax.random.fold_in(key_list[10], 71), 0)
    sink_counts = draw_sink_counts(jax.random.fold_in(key_list[10], 71), 0)
    windows = draw_windows(jax.random.fold_in(key_list[10], 71), 0)
    block_of_slot = jax.vmap(lambda own: jax.random.permutation(own, N_SEQ))(jax.random.split(key_list[9], REQUESTS)).reshape((REQUESTS, N_SEQ)).astype(jnp.int32)
    return dict(query=query, span_keys=span_keys, span_values=span_values, cache_keys=cache_keys, cache_values=cache_values, out_weight=out_weight, cache_lengths=cache_lengths, sink_counts=sink_counts, windows=windows, block_of_slot=block_of_slot)


NEG = -1e+30

def visible(query_pos, key_pos, valid, window, sinks):
    later = query_pos[:, None]
    earlier = key_pos[None, :]
    near = later - earlier < window
    return (earlier <= later) & (near | (earlier < sinks)) & valid[None, :]

def reference(query, span_keys, span_values, cache_keys, cache_values, out_weight, cache_lengths, sink_counts, windows, block_of_slot):
    scale = 1.0 / math.sqrt(HEAD)
    query_grid = query.reshape(GROUP, REQUESTS, Q_DEV, D)
    keys_grid = span_keys.reshape(GROUP, REQUESTS, Q_DEV, D)
    vals_grid = span_values.reshape(GROUP, REQUESTS, Q_DEV, D)

    def one_request(r):
        q_rows = lax.dynamic_index_in_dim(query_grid, r, 1, keepdims=False).reshape(SPAN, HEADS, HEAD)
        c_keys = lax.dynamic_index_in_dim(keys_grid, r, 1, keepdims=False).reshape(SPAN, D)
        c_vals = lax.dynamic_index_in_dim(vals_grid, r, 1, keepdims=False).reshape(SPAN, D)
        all_keys = jnp.concatenate([cache_keys[r], c_keys], 0).reshape(-1, HEADS, HEAD)
        all_vals = jnp.concatenate([cache_values[r], c_vals], 0).reshape(-1, HEADS, HEAD)
        length = cache_lengths[r]
        slot_pos = (block_of_slot[r][:, None] * CACHE_DEV + jnp.arange(CACHE_DEV, dtype=jnp.int32)[None, :]).reshape(-1).astype(jnp.int32)
        span_pos = (length + jnp.arange(SPAN, dtype=jnp.int32)).astype(jnp.int32)
        key_pos = jnp.concatenate([slot_pos, span_pos])
        valid = jnp.concatenate([slot_pos < length, jnp.ones((SPAN,), jnp.bool_)])
        mask = visible(span_pos, key_pos, valid, windows[r], sink_counts[r])

        def one_head(h):
            q_head = q_rows[:, h]
            k_head = all_keys[:, h]
            v_head = all_vals[:, h]
            scores = jnp.dot(q_head, k_head.T, preferred_element_type=jnp.float32) * scale
            scores = jnp.where(mask, scores, NEG)
            top = lax.optimization_barrier(jnp.max(scores, axis=1, keepdims=True))
            weights = jnp.where(mask, jnp.exp(scores - top), 0.0)
            total = lax.optimization_barrier(jnp.sum(weights, axis=1, keepdims=True))
            summed = jnp.dot(weights.astype(jnp.bfloat16), v_head, preferred_element_type=jnp.float32)
            return (summed / total).astype(jnp.bfloat16)
        per_head = lax.map(one_head, jnp.arange(HEADS, dtype=jnp.int32))
        return jnp.transpose(per_head, (1, 0, 2)).reshape(SPAN, D)
    attention = lax.map(one_request, jnp.arange(REQUESTS, dtype=jnp.int32))
    attention = jnp.transpose(attention.reshape(REQUESTS, GROUP, Q_DEV, D), (1, 0, 2, 3)).reshape(TOKENS, D)
    return jnp.dot(attention, out_weight, preferred_element_type=jnp.float32).astype(jnp.bfloat16)
```

```python
import math

import jax
import jax.numpy as jnp
import numpy as np
from jax import lax
from jax.sharding import Mesh
from jax.sharding import PartitionSpec as P

HEAD = 128
GROUP = 4


NEG = -1e30


def visible(query_pos, key_pos, valid, window, sinks):
    later = query_pos[:, None]
    earlier = key_pos[None, :]
    near = later - earlier < window
    return (earlier <= later) & (near | (earlier < sinks)) & valid[None, :]


def block_partial(q_rows, keys, vals, query_pos, key_pos, valid, window, sinks):
    mask = visible(query_pos, key_pos, valid, window, sinks)
    scale = 1.0 / math.sqrt(q_rows.shape[-1])
    scores = jnp.einsum("qhd,khd->hqk", q_rows, keys, preferred_element_type=jnp.float32) * scale
    scores = jnp.where(mask[None], scores, NEG)
    top = jnp.max(scores, axis=2)
    weights = jnp.where(mask[None], jnp.exp(scores - top[:, :, None]), 0.0)
    total = jnp.sum(weights, axis=2)
    summed = jnp.einsum(
        "hqk,khd->qhd", weights.astype(jnp.bfloat16), vals, preferred_element_type=jnp.float32
    )
    return (summed, top.T, total.T)


def shards(
    query,
    span_keys,
    span_values,
    cache_keys,
    cache_values,
    out_weight,
    cache_lengths,
    sink_counts,
    windows,
    block_of_slot,
):
    rows, width = query.shape
    heads_here = width // HEAD
    places = lax.axis_size("place")
    group = lax.axis_size("req")
    place = lax.axis_index("place")
    mine = lax.axis_index("req")
    cache_dev = cache_keys.shape[1]
    length = cache_lengths[mine]
    window = windows[mine]
    sinks = sink_counts[mine]

    got_keys = lax.all_to_all(cache_keys, "req", split_axis=0, concat_axis=0, tiled=True)
    got_vals = lax.all_to_all(cache_values, "req", split_axis=0, concat_axis=0, tiled=True)
    span_q = lax.all_gather(query, "place", axis=0, tiled=True)

    blocks = lax.dynamic_slice_in_dim(block_of_slot[mine], place * group, group)
    slot_pos = (blocks[:, None] * cache_dev + jnp.arange(cache_dev, dtype=jnp.int32)[None, :]).reshape(-1)
    own_pos = length + place * rows + jnp.arange(rows, dtype=jnp.int32)
    query_pos = length + jnp.arange(places * rows, dtype=jnp.int32)

    keys = jnp.concatenate([got_keys.reshape(-1, width), span_keys], 0).reshape(-1, heads_here, HEAD)
    vals = jnp.concatenate([got_vals.reshape(-1, width), span_values], 0).reshape(-1, heads_here, HEAD)
    key_pos = jnp.concatenate([slot_pos, own_pos])
    valid = jnp.concatenate([slot_pos < length, jnp.ones((rows,), jnp.bool_)])

    summed, top, total = block_partial(
        span_q.reshape(-1, heads_here, HEAD), keys, vals, query_pos, key_pos, valid, window, sinks
    )
    summed = lax.all_to_all(
        summed.reshape(places, rows, width), "place", split_axis=0, concat_axis=0, tiled=True
    ).reshape(places, rows, heads_here, HEAD)
    stats = jnp.concatenate([top, total], axis=1).reshape(places, rows, 2 * heads_here)
    stats = lax.all_to_all(stats, "place", split_axis=0, concat_axis=0, tiled=True)
    top, total = stats[..., :heads_here], stats[..., heads_here:]
    best = jnp.max(top, axis=0)
    factor = jnp.exp(top - best[None])
    total = jnp.sum(total * factor, axis=0)
    summed = jnp.sum(summed * factor[..., None], axis=0)
    attention = (summed / total[..., None]).astype(jnp.bfloat16).reshape(rows, width)
    terms = jnp.dot(attention, out_weight, preferred_element_type=jnp.float32)
    return lax.psum_scatter(terms.astype(jnp.bfloat16), "tp", scatter_dimension=1, tiled=True)


def solution(mesh):
    seq_size = mesh.shape["seq"]
    requests = 8
    grid = Mesh(
        np.asarray(mesh.devices).reshape(seq_size // requests, requests, mesh.shape["tp"]),
        ("place", "req", "tp"),
    )
    seq = ("place", "req")
    return jax.shard_map(
        shards,
        mesh=grid,
        in_specs=(
            P(seq, "tp"),
            P(seq, "tp"),
            P(seq, "tp"),
            P(None, seq, "tp"),
            P(None, seq, "tp"),
            P("tp", None),
            P(),
            P(),
            P(),
            P(),
        ),
        out_specs=P(seq, "tp"),
        check_vma=False,
    )
```

```python
import math

import jax
import jax.numpy as jnp
import numpy as np
from jax import lax
from jax.sharding import Mesh
from jax.sharding import PartitionSpec as P

HEAD = 128
GROUP = 4


NEG = -1e30


def visible(query_pos, key_pos, valid, window, sinks):
    later = query_pos[:, None]
    earlier = key_pos[None, :]
    near = later - earlier < window
    return (earlier <= later) & (near | (earlier < sinks)) & valid[None, :]


def block_partial(q_rows, keys, vals, query_pos, key_pos, valid, window, sinks):
    mask = visible(query_pos, key_pos, valid, window, sinks)
    scale = 1.0 / math.sqrt(q_rows.shape[-1])
    scores = jnp.einsum("qhd,khd->hqk", q_rows, keys, preferred_element_type=jnp.float32) * scale
    scores = jnp.where(mask[None], scores, NEG)
    top = jnp.max(scores, axis=2)
    weights = jnp.where(mask[None], jnp.exp(scores - top[:, :, None]), 0.0)
    total = jnp.sum(weights, axis=2)
    summed = jnp.einsum(
        "hqk,khd->qhd", weights.astype(jnp.bfloat16), vals, preferred_element_type=jnp.float32
    )
    return (summed, top.T, total.T)


def shards(
    query,
    span_keys,
    span_values,
    cache_keys,
    cache_values,
    out_weight,
    cache_lengths,
    sink_counts,
    windows,
    block_of_slot,
):
    rows, width = query.shape
    heads_here = width // HEAD
    places = lax.axis_size("place")
    group = lax.axis_size("req")
    place = lax.axis_index("place")
    mine = lax.axis_index("req")
    cache_dev = cache_keys.shape[1]
    length = cache_lengths[mine]
    window = windows[mine]
    sinks = sink_counts[mine]

    got_keys = lax.all_to_all(cache_keys, "req", split_axis=0, concat_axis=0, tiled=True)
    got_vals = lax.all_to_all(cache_values, "req", split_axis=0, concat_axis=0, tiled=True)
    span_q = lax.all_to_all(
        jnp.broadcast_to(query[None], (places,) + query.shape), "place", split_axis=0, concat_axis=0, tiled=True
    )

    blocks = lax.dynamic_slice_in_dim(block_of_slot[mine], place * group, group)
    slot_pos = (blocks[:, None] * cache_dev + jnp.arange(cache_dev, dtype=jnp.int32)[None, :]).reshape(-1)
    own_pos = length + place * rows + jnp.arange(rows, dtype=jnp.int32)
    query_pos = length + jnp.arange(places * rows, dtype=jnp.int32)

    keys = jnp.concatenate([got_keys.reshape(-1, width), span_keys], 0).reshape(-1, heads_here, HEAD)
    vals = jnp.concatenate([got_vals.reshape(-1, width), span_values], 0).reshape(-1, heads_here, HEAD)
    key_pos = jnp.concatenate([slot_pos, own_pos])
    valid = jnp.concatenate([slot_pos < length, jnp.ones((rows,), jnp.bool_)])

    summed, top, total = block_partial(
        span_q.reshape(-1, heads_here, HEAD), keys, vals, query_pos, key_pos, valid, window, sinks
    )
    summed = lax.all_to_all(
        summed.reshape(places, rows, width), "place", split_axis=0, concat_axis=0, tiled=True
    ).reshape(places, rows, heads_here, HEAD)
    stats = jnp.concatenate([top, total], axis=1).reshape(places, rows, 2 * heads_here)
    stats = lax.all_to_all(stats, "place", split_axis=0, concat_axis=0, tiled=True)
    top, total = stats[..., :heads_here], stats[..., heads_here:]
    best = jnp.max(top, axis=0)
    factor = jnp.exp(top - best[None])
    total = jnp.sum(total * factor, axis=0)
    summed = jnp.sum(summed * factor[..., None], axis=0)
    attention = (summed / total[..., None]).astype(jnp.bfloat16).reshape(rows, width)
    parts = lax.axis_size("tp")
    terms = jnp.einsum(
        "qf,fkc->kqc", attention, out_weight.reshape(width, parts, -1), preferred_element_type=jnp.float32
    )
    terms = lax.all_to_all(terms.astype(jnp.bfloat16), "tp", split_axis=0, concat_axis=0, tiled=True)
    return jnp.sum(terms.astype(jnp.float32), axis=0).astype(jnp.bfloat16)


def solution(mesh):
    seq_size = mesh.shape["seq"]
    requests = 8
    grid = Mesh(
        np.asarray(mesh.devices).reshape(seq_size // requests, requests, mesh.shape["tp"]),
        ("place", "req", "tp"),
    )
    seq = ("place", "req")
    return jax.shard_map(
        shards,
        mesh=grid,
        in_specs=(
            P(seq, "tp"),
            P(seq, "tp"),
            P(seq, "tp"),
            P(None, seq, "tp"),
            P(None, seq, "tp"),
            P("tp", None),
            P(),
            P(),
            P(),
            P(),
        ),
        out_specs=P(seq, "tp"),
        check_vma=False,
    )
```

```python
import math

import jax
import jax.numpy as jnp
import numpy as np
from jax import lax
from jax.sharding import Mesh
from jax.sharding import PartitionSpec as P

HEAD = 128
GROUP = 4


NEG = -1e30


def visible(query_pos, key_pos, valid, window, sinks):
    later = query_pos[:, None]
    earlier = key_pos[None, :]
    near = later - earlier < window
    return (earlier <= later) & (near | (earlier < sinks)) & valid[None, :]


def block_partial(q_rows, keys, vals, query_pos, key_pos, valid, window, sinks):
    mask = visible(query_pos, key_pos, valid, window, sinks)
    scale = 1.0 / math.sqrt(q_rows.shape[-1])
    scores = jnp.einsum("qhd,khd->hqk", q_rows, keys, preferred_element_type=jnp.float32) * scale
    scores = jnp.where(mask[None], scores, NEG)
    top = jnp.max(scores, axis=2)
    weights = jnp.where(mask[None], jnp.exp(scores - top[:, :, None]), 0.0)
    total = jnp.sum(weights, axis=2)
    summed = jnp.einsum(
        "hqk,khd->qhd", weights.astype(jnp.bfloat16), vals, preferred_element_type=jnp.float32
    )
    return (summed, top.T, total.T)


def shards(
    query,
    span_keys,
    span_values,
    cache_keys,
    cache_values,
    out_weight,
    cache_lengths,
    sink_counts,
    windows,
    block_of_slot,
):
    rows, width = query.shape
    heads_here = width // HEAD
    places = lax.axis_size("place")
    group = lax.axis_size("req")
    place = lax.axis_index("place")
    mine = lax.axis_index("req")
    cache_dev = cache_keys.shape[1]
    length = cache_lengths[mine]
    window = windows[mine]
    sinks = sink_counts[mine]

    got_keys = lax.all_to_all(cache_keys, "req", split_axis=0, concat_axis=0, tiled=True)
    got_vals = lax.all_to_all(cache_values, "req", split_axis=0, concat_axis=0, tiled=True)
    span_q = lax.all_to_all(
        jnp.broadcast_to(query[None], (places,) + query.shape), "place", split_axis=0, concat_axis=0, tiled=True
    )

    blocks = lax.dynamic_slice_in_dim(block_of_slot[mine], place * group, group)
    slot_pos = (blocks[:, None] * cache_dev + jnp.arange(cache_dev, dtype=jnp.int32)[None, :]).reshape(-1)
    own_pos = length + place * rows + jnp.arange(rows, dtype=jnp.int32)
    query_pos = length + jnp.arange(places * rows, dtype=jnp.int32)

    keys = jnp.concatenate([got_keys.reshape(-1, width), span_keys], 0).reshape(-1, heads_here, HEAD)
    vals = jnp.concatenate([got_vals.reshape(-1, width), span_values], 0).reshape(-1, heads_here, HEAD)
    key_pos = jnp.concatenate([slot_pos, own_pos])
    valid = jnp.concatenate([slot_pos < length, jnp.ones((rows,), jnp.bool_)])

    summed, top, total = block_partial(
        span_q.reshape(-1, heads_here, HEAD), keys, vals, query_pos, key_pos, valid, window, sinks
    )
    summed = lax.all_to_all(
        summed.astype(jnp.bfloat16).reshape(places, rows, width), "place", split_axis=0, concat_axis=0, tiled=True
    ).reshape(places, rows, heads_here, HEAD).astype(jnp.float32)
    stats = jnp.concatenate([top, total], axis=1).reshape(places, rows, 2 * heads_here)
    stats = lax.all_to_all(stats, "place", split_axis=0, concat_axis=0, tiled=True)
    top, total = stats[..., :heads_here], stats[..., heads_here:]
    best = jnp.max(top, axis=0)
    factor = jnp.exp(top - best[None])
    total = jnp.sum(total * factor, axis=0)
    summed = jnp.sum(summed * factor[..., None], axis=0)
    attention = (summed / total[..., None]).astype(jnp.bfloat16).reshape(rows, width)
    parts = lax.axis_size("tp")
    terms = jnp.einsum(
        "qf,fkc->kqc", attention, out_weight.reshape(width, parts, -1), preferred_element_type=jnp.float32
    )
    terms = lax.all_to_all(terms.astype(jnp.bfloat16), "tp", split_axis=0, concat_axis=0, tiled=True)
    return jnp.sum(terms.astype(jnp.float32), axis=0).astype(jnp.bfloat16)


def solution(mesh):
    seq_size = mesh.shape["seq"]
    requests = 8
    grid = Mesh(
        np.asarray(mesh.devices).reshape(seq_size // requests, requests, mesh.shape["tp"]),
        ("place", "req", "tp"),
    )
    seq = ("place", "req")
    return jax.shard_map(
        shards,
        mesh=grid,
        in_specs=(
            P(seq, "tp"),
            P(seq, "tp"),
            P(seq, "tp"),
            P(None, seq, "tp"),
            P(None, seq, "tp"),
            P("tp", None),
            P(),
            P(),
            P(),
            P(),
        ),
        out_specs=P(seq, "tp"),
        check_vma=False,
    )
```

```python
import math

import jax
import jax.numpy as jnp
import numpy as np
from jax import lax
from jax.sharding import Mesh
from jax.sharding import PartitionSpec as P

HEAD = 128
GROUP = 4


NEG = -1e30


def visible(query_pos, key_pos, valid, window, sinks):
    later = query_pos[:, None]
    earlier = key_pos[None, :]
    near = later - earlier < window
    return (earlier <= later) & (near | (earlier < sinks)) & valid[None, :]


def block_partial(q_rows, keys, vals, query_pos, key_pos, valid, window, sinks):
    mask = visible(query_pos, key_pos, valid, window, sinks)
    scale = 1.0 / math.sqrt(q_rows.shape[-1])
    scores = jnp.einsum("qhd,khd->hqk", q_rows, keys, preferred_element_type=jnp.float32) * scale
    scores = jnp.where(mask[None], scores, NEG)
    top = jnp.max(scores, axis=2)
    weights = jnp.where(mask[None], jnp.exp(scores - top[:, :, None]), 0.0)
    total = jnp.sum(weights, axis=2)
    summed = jnp.einsum(
        "hqk,khd->qhd", weights.astype(jnp.bfloat16), vals, preferred_element_type=jnp.float32
    )
    return (summed, top.T, total.T)


def shards(
    query,
    span_keys,
    span_values,
    cache_keys,
    cache_values,
    out_weight,
    cache_lengths,
    sink_counts,
    windows,
    block_of_slot,
):
    rows, width = query.shape
    heads_here = width // HEAD
    places = lax.axis_size("place")
    group = lax.axis_size("req")
    devices = places * group
    place = lax.axis_index("place")
    mine = lax.axis_index("req")
    me = place * group + mine
    cache_dev = cache_keys.shape[1]
    length = cache_lengths[mine]
    window = windows[mine]
    sinks = sink_counts[mine]
    seq = ("place", "req")

    ring = devices // 4
    core, z, y = me % 2, (me // 2) % ring, me // (2 * ring)

    def at(yy, zz, cc):
        return (yy * ring + zz % ring) * 2 + cc

    def request_of(index):
        return index % group

    moves = [(d, flip) for d in (-1, 0, 1) for flip in (0, 1)] + [("far", c) for c in (0, 1)]
    got_keys, got_vals, got_slot = [], [], []
    for d, flip in moves:
        if d == "far":
            target = jnp.where(core == 0, at(y, z + 2, flip), at(y, z - 2, 1 - flip))
            source = jnp.where(core == flip, at(y, z - 2, 0), at(y, z + 2, 1))
            pairs = []
            for s_idx in range(devices):
                sc, sz, sy = s_idx % 2, (s_idx // 2) % ring, s_idx // (2 * ring)
                if sc == 0:
                    pairs.append((s_idx, (sy * ring + (sz + 2) % ring) * 2 + flip))
                else:
                    pairs.append((s_idx, (sy * ring + (sz - 2) % ring) * 2 + 1 - flip))
        else:
            target = at(y, z + d, core ^ flip)
            source = at(y, z - d, core ^ flip)
            pairs = []
            for s_idx in range(devices):
                sc, sz, sy = s_idx % 2, (s_idx // 2) % ring, s_idx // (2 * ring)
                pairs.append((s_idx, (sy * ring + (sz + d) % ring) * 2 + (sc ^ flip)))
        sent = request_of(target)
        chunk = (
            lax.dynamic_index_in_dim(cache_keys, sent, 0, keepdims=False),
            lax.dynamic_index_in_dim(cache_values, sent, 0, keepdims=False),
        )
        if d != 0 or flip != 0:
            chunk = lax.ppermute(chunk, seq, pairs)
        got_keys.append(chunk[0])
        got_vals.append(chunk[1])
        got_slot.append(source)

    span_q = [query]
    for k in range(1, places):
        pairs = [(p * group + i, ((p + k) % places) * group + i) for p in range(places) for i in range(group)]
        span_q.append(lax.ppermute(query, seq, pairs))
    span_q = jnp.stack(span_q)
    from_place = (place - jnp.arange(places, dtype=jnp.int32)) % places

    slots = jnp.stack(got_slot)
    blocks = block_of_slot[mine][slots]
    slot_pos = (blocks[:, None] * cache_dev + jnp.arange(cache_dev, dtype=jnp.int32)[None, :]).reshape(-1)
    own_pos = length + place * rows + jnp.arange(rows, dtype=jnp.int32)
    query_pos = (length + from_place[:, None] * rows + jnp.arange(rows, dtype=jnp.int32)[None, :]).reshape(-1)

    keys = jnp.concatenate(got_keys + [span_keys], 0).reshape(-1, heads_here, HEAD)
    vals = jnp.concatenate(got_vals + [span_values], 0).reshape(-1, heads_here, HEAD)
    key_pos = jnp.concatenate([slot_pos, own_pos])
    valid = jnp.concatenate([slot_pos < length, jnp.ones((rows,), jnp.bool_)])

    summed, top, total = block_partial(
        span_q.reshape(-1, heads_here, HEAD), keys, vals, query_pos, key_pos, valid, window, sinks
    )
    summed = summed.astype(jnp.bfloat16).reshape(places, rows, width)
    stats = jnp.concatenate([top, total], axis=1).reshape(places, rows, 2 * heads_here)
    back_sum, back_stats = [summed[0]], [stats[0]]
    for k in range(1, places):
        pairs = [(p * group + i, ((p - k) % places) * group + i) for p in range(places) for i in range(group)]
        got = lax.ppermute((summed[k], stats[k]), seq, pairs)
        back_sum.append(got[0])
        back_stats.append(got[1])
    summed = jnp.stack(back_sum).astype(jnp.float32).reshape(places, rows, heads_here, HEAD)
    stats = jnp.stack(back_stats)
    top, total = stats[..., :heads_here], stats[..., heads_here:]
    best = jnp.max(top, axis=0)
    factor = jnp.exp(top - best[None])
    total = jnp.sum(total * factor, axis=0)
    summed = jnp.sum(summed * factor[..., None], axis=0)
    attention = (summed / total[..., None]).astype(jnp.bfloat16).reshape(rows, width)
    parts = lax.axis_size("tp")
    terms = jnp.einsum(
        "qf,fkc->kqc", attention, out_weight.reshape(width, parts, -1), preferred_element_type=jnp.float32
    )
    terms = lax.all_to_all(terms.astype(jnp.bfloat16), "tp", split_axis=0, concat_axis=0, tiled=True)
    return jnp.sum(terms.astype(jnp.float32), axis=0).astype(jnp.bfloat16)


def solution(mesh):
    seq_size = mesh.shape["seq"]
    requests = 8
    grid = Mesh(
        np.asarray(mesh.devices).reshape(seq_size // requests, requests, mesh.shape["tp"]),
        ("place", "req", "tp"),
    )
    seq = ("place", "req")
    return jax.shard_map(
        shards,
        mesh=grid,
        in_specs=(
            P(seq, "tp"),
            P(seq, "tp"),
            P(seq, "tp"),
            P(None, seq, "tp"),
            P(None, seq, "tp"),
            P("tp", None),
            P(),
            P(),
            P(),
            P(),
        ),
        out_specs=P(seq, "tp"),
        check_vma=False,
    )
```

```python
import math

import jax
import jax.numpy as jnp
import numpy as np
from jax import lax
from jax.sharding import Mesh
from jax.sharding import PartitionSpec as P

HEAD = 128
GROUP = 4


NEG = -1e30


def visible(query_pos, key_pos, valid, window, sinks):
    later = query_pos[:, None]
    earlier = key_pos[None, :]
    near = later - earlier < window
    return (earlier <= later) & (near | (earlier < sinks)) & valid[None, :]


def block_partial(q_rows, keys, vals, query_pos, key_pos, valid, window, sinks):
    mask = visible(query_pos, key_pos, valid, window, sinks)
    scale = 1.0 / math.sqrt(q_rows.shape[-1])
    scores = jnp.einsum("qhd,khd->hqk", q_rows, keys, preferred_element_type=jnp.float32) * scale
    scores = jnp.where(mask[None], scores, NEG)
    top = jnp.max(scores, axis=2)
    weights = jnp.where(mask[None], jnp.exp(scores - top[:, :, None]), 0.0)
    total = jnp.sum(weights, axis=2)
    summed = jnp.einsum(
        "hqk,khd->qhd", weights.astype(jnp.bfloat16), vals, preferred_element_type=jnp.float32
    )
    return (summed, top.T, total.T)


def shards(
    query,
    span_keys,
    span_values,
    cache_keys,
    cache_values,
    out_weight,
    cache_lengths,
    sink_counts,
    windows,
    block_of_slot,
):
    rows, width = query.shape
    heads_here = width // HEAD
    places = lax.axis_size("place")
    group = lax.axis_size("req")
    devices = places * group
    place = lax.axis_index("place")
    mine = lax.axis_index("req")
    me = place * group + mine
    cache_dev = cache_keys.shape[1]
    length = cache_lengths[mine]
    window = windows[mine]
    sinks = sink_counts[mine]
    seq = ("place", "req")

    ring = devices // 4
    core, z, y = me % 2, (me // 2) % ring, me // (2 * ring)

    def at(yy, zz, cc):
        return (yy * ring + zz % ring) * 2 + cc

    def request_of(index):
        return index % group

    moves = [(d, flip) for d in (-1, 0, 1) for flip in (0, 1)] + [("far", c) for c in (0, 1)]
    got_keys, got_vals, got_slot = [], [], []
    for d, flip in moves:
        if d == "far":
            target = jnp.where(core == 0, at(y, z + 2, flip), at(y, z - 2, 1 - flip))
            source = jnp.where(core == flip, at(y, z - 2, 0), at(y, z + 2, 1))
            pairs = []
            for s_idx in range(devices):
                sc, sz, sy = s_idx % 2, (s_idx // 2) % ring, s_idx // (2 * ring)
                if sc == 0:
                    pairs.append((s_idx, (sy * ring + (sz + 2) % ring) * 2 + flip))
                else:
                    pairs.append((s_idx, (sy * ring + (sz - 2) % ring) * 2 + 1 - flip))
        else:
            target = at(y, z + d, core ^ flip)
            source = at(y, z - d, core ^ flip)
            pairs = []
            for s_idx in range(devices):
                sc, sz, sy = s_idx % 2, (s_idx // 2) % ring, s_idx // (2 * ring)
                pairs.append((s_idx, (sy * ring + (sz + d) % ring) * 2 + (sc ^ flip)))
        sent = request_of(target)
        chunk = jnp.stack(
            [
                lax.dynamic_index_in_dim(cache_keys, sent, 0, keepdims=False),
                lax.dynamic_index_in_dim(cache_values, sent, 0, keepdims=False),
            ]
        )
        if d != 0 or flip != 0:
            chunk = lax.ppermute(chunk, seq, pairs)
        got_keys.append(chunk[0])
        got_vals.append(chunk[1])
        got_slot.append(source)

    span_q = [query]
    for k in range(1, places):
        pairs = [(p * group + i, ((p + k) % places) * group + i) for p in range(places) for i in range(group)]
        span_q.append(lax.ppermute(query, seq, pairs))
    span_q = jnp.stack(span_q)
    from_place = (place - jnp.arange(places, dtype=jnp.int32)) % places

    slots = jnp.stack(got_slot)
    blocks = block_of_slot[mine][slots]
    slot_pos = (blocks[:, None] * cache_dev + jnp.arange(cache_dev, dtype=jnp.int32)[None, :]).reshape(-1)
    own_pos = length + place * rows + jnp.arange(rows, dtype=jnp.int32)
    query_pos = (length + from_place[:, None] * rows + jnp.arange(rows, dtype=jnp.int32)[None, :]).reshape(-1)

    keys = jnp.concatenate(got_keys + [span_keys], 0).reshape(-1, heads_here, HEAD)
    vals = jnp.concatenate(got_vals + [span_values], 0).reshape(-1, heads_here, HEAD)
    key_pos = jnp.concatenate([slot_pos, own_pos])
    valid = jnp.concatenate([slot_pos < length, jnp.ones((rows,), jnp.bool_)])

    summed, top, total = block_partial(
        span_q.reshape(-1, heads_here, HEAD), keys, vals, query_pos, key_pos, valid, window, sinks
    )
    summed = summed.astype(jnp.bfloat16).reshape(places, rows, width)
    stats = jnp.concatenate([top, total], axis=1).reshape(places, rows, 2 * heads_here)
    back_sum, back_stats = [summed[0]], [stats[0]]
    for k in range(1, places):
        pairs = [(p * group + i, ((p - k) % places) * group + i) for p in range(places) for i in range(group)]
        got = lax.ppermute((summed[k], stats[k]), seq, pairs)
        back_sum.append(got[0])
        back_stats.append(got[1])
    summed = jnp.stack(back_sum).astype(jnp.float32).reshape(places, rows, heads_here, HEAD)
    stats = jnp.stack(back_stats)
    top, total = stats[..., :heads_here], stats[..., heads_here:]
    best = jnp.max(top, axis=0)
    factor = jnp.exp(top - best[None])
    total = jnp.sum(total * factor, axis=0)
    summed = jnp.sum(summed * factor[..., None], axis=0)
    attention = (summed / total[..., None]).astype(jnp.bfloat16).reshape(rows, width)
    parts = lax.axis_size("tp")
    terms = jnp.einsum(
        "qf,fkc->kqc", attention, out_weight.reshape(width, parts, -1), preferred_element_type=jnp.float32
    )
    terms = lax.all_to_all(terms.astype(jnp.bfloat16), "tp", split_axis=0, concat_axis=0, tiled=True)
    return jnp.sum(terms.astype(jnp.float32), axis=0).astype(jnp.bfloat16)


def solution(mesh):
    seq_size = mesh.shape["seq"]
    requests = 8
    grid = Mesh(
        np.asarray(mesh.devices).reshape(seq_size // requests, requests, mesh.shape["tp"]),
        ("place", "req", "tp"),
    )
    seq = ("place", "req")
    return jax.shard_map(
        shards,
        mesh=grid,
        in_specs=(
            P(seq, "tp"),
            P(seq, "tp"),
            P(seq, "tp"),
            P(None, seq, "tp"),
            P(None, seq, "tp"),
            P("tp", None),
            P(),
            P(),
            P(),
            P(),
        ),
        out_specs=P(seq, "tp"),
        check_vma=False,
    )
```

```python
import math

import jax
import jax.numpy as jnp
import numpy as np
from jax import lax
from jax.experimental import pallas as pl
from jax.experimental.pallas import tpu as pltpu
from jax.sharding import Mesh
from jax.sharding import PartitionSpec as P

HEAD = 128
GROUP = 4


NEG = -1e30


def attend(q_rows, chunks, span_k, span_v, params, places, interpret=False):
    total_rows, width = q_rows.shape
    rows = total_rows // places
    heads = width // HEAD
    n = len(chunks)
    cdev = chunks[0].shape[1]
    srows = span_k.shape[0]
    scale = 1.0 / math.sqrt(HEAD)

    def kernel(par, q_ref, *refs):
        kv_refs = refs[:n]
        sk_ref, sv_ref, o_ref, m_ref, l_ref = refs[n:]
        k = pl.program_id(1)
        length = par[n + 1]
        window = par[n + 2]
        sinks = par[n + 3]
        qpos = par[n + 4 + k] + lax.broadcasted_iota(jnp.int32, (rows, 1), 0)
        q = q_ref[...]
        m = jnp.full((rows, 1), NEG, jnp.float32)
        l = jnp.zeros((rows, 1), jnp.float32)
        acc = jnp.zeros((rows, HEAD), jnp.float32)
        for c in range(n + 1):
            if c < n:
                keys = kv_refs[c][0]
                vals = kv_refs[c][1]
                kpos = par[c] + lax.broadcasted_iota(jnp.int32, (1, cdev), 1)
                valid = kpos < length
            else:
                keys = sk_ref[...]
                vals = sv_ref[...]
                kpos = par[n] + lax.broadcasted_iota(jnp.int32, (1, srows), 1)
                valid = kpos >= 0
            s = lax.dot_general(q, keys, (((1,), (1,)), ((), ())), preferred_element_type=jnp.float32) * scale
            mask = (kpos <= qpos) & ((qpos - kpos < window) | (kpos < sinks)) & valid
            s = jnp.where(mask, s, NEG)
            m_new = jnp.maximum(m, jnp.max(s, axis=1, keepdims=True))
            alpha = jnp.exp(m - m_new)
            p = jnp.where(mask, jnp.exp(s - m_new), 0.0)
            l = alpha * l + jnp.sum(p, axis=1, keepdims=True)
            acc = alpha * acc + jnp.dot(p.astype(jnp.bfloat16), vals, preferred_element_type=jnp.float32)
            m = m_new
        o_ref[...] = acc.astype(o_ref.dtype)
        m_ref[...] = m
        l_ref[...] = l

    in_specs = [pl.BlockSpec((rows, HEAD), lambda h, k, par: (k, h))]
    in_specs += [pl.BlockSpec((2, cdev, HEAD), lambda h, k, par: (0, 0, h)) for _ in range(n)]
    in_specs += [pl.BlockSpec((srows, HEAD), lambda h, k, par: (0, h))] * 2
    out_specs = [
        pl.BlockSpec((rows, HEAD), lambda h, k, par: (k, h)),
        pl.BlockSpec((None, rows, 1), lambda h, k, par: (h, k, 0)),
        pl.BlockSpec((None, rows, 1), lambda h, k, par: (h, k, 0)),
    ]
    out_shape = [
        jax.ShapeDtypeStruct((total_rows, width), jnp.bfloat16),
        jax.ShapeDtypeStruct((heads, total_rows, 1), jnp.float32),
        jax.ShapeDtypeStruct((heads, total_rows, 1), jnp.float32),
    ]
    return pl.pallas_call(
        kernel,
        grid_spec=pltpu.PrefetchScalarGridSpec(
            num_scalar_prefetch=1, grid=(heads, places), in_specs=in_specs, out_specs=out_specs
        ),
        out_shape=out_shape,
        interpret=interpret,
    )(params, q_rows, *chunks, span_k, span_v)


def shards(
    query,
    span_keys,
    span_values,
    cache_keys,
    cache_values,
    out_weight,
    cache_lengths,
    sink_counts,
    windows,
    block_of_slot,
):
    rows, width = query.shape
    heads_here = width // HEAD
    places = lax.axis_size("place")
    group = lax.axis_size("req")
    devices = places * group
    place = lax.axis_index("place")
    mine = lax.axis_index("req")
    me = place * group + mine
    cache_dev = cache_keys.shape[1]
    length = cache_lengths[mine]
    window = windows[mine]
    sinks = sink_counts[mine]
    seq = ("place", "req")

    ring = devices // 4
    core, z, y = me % 2, (me // 2) % ring, me // (2 * ring)

    def at(yy, zz, cc):
        return (yy * ring + zz % ring) * 2 + cc

    def request_of(index):
        return index % group

    moves = [(d, flip) for d in (-1, 0, 1) for flip in (0, 1)] + [("far", c) for c in (0, 1)]
    got_kv, got_slot = [], []
    for d, flip in moves:
        if d == "far":
            target = jnp.where(core == 0, at(y, z + 2, flip), at(y, z - 2, 1 - flip))
            source = jnp.where(core == flip, at(y, z - 2, 0), at(y, z + 2, 1))
            pairs = []
            for s_idx in range(devices):
                sc, sz, sy = s_idx % 2, (s_idx // 2) % ring, s_idx // (2 * ring)
                if sc == 0:
                    pairs.append((s_idx, (sy * ring + (sz + 2) % ring) * 2 + flip))
                else:
                    pairs.append((s_idx, (sy * ring + (sz - 2) % ring) * 2 + 1 - flip))
        else:
            target = at(y, z + d, core ^ flip)
            source = at(y, z - d, core ^ flip)
            pairs = []
            for s_idx in range(devices):
                sc, sz, sy = s_idx % 2, (s_idx // 2) % ring, s_idx // (2 * ring)
                pairs.append((s_idx, (sy * ring + (sz + d) % ring) * 2 + (sc ^ flip)))
        sent = request_of(target)
        chunk = jnp.stack(
            [
                lax.dynamic_index_in_dim(cache_keys, sent, 0, keepdims=False),
                lax.dynamic_index_in_dim(cache_values, sent, 0, keepdims=False),
            ]
        )
        if d != 0 or flip != 0:
            chunk = lax.ppermute(chunk, seq, pairs)
        got_kv.append(chunk)
        got_slot.append(source)

    span_q = [query]
    for k in range(1, places):
        pairs = [(p * group + i, ((p + k) % places) * group + i) for p in range(places) for i in range(group)]
        span_q.append(lax.ppermute(query, seq, pairs))
    span_q = jnp.stack(span_q)
    from_place = (place - jnp.arange(places, dtype=jnp.int32)) % places

    slots = jnp.stack(got_slot)
    blocks = block_of_slot[mine][slots]
    params = jnp.concatenate(
        [
            blocks * cache_dev,
            jnp.stack([length + place * rows, length, window, sinks]),
            length + from_place * rows,
        ]
    ).astype(jnp.int32)
    summed, top, total = attend(span_q.reshape(-1, width), got_kv, span_keys, span_values, params, places)
    summed = summed.reshape(places, rows, width)
    stats = jnp.concatenate([top[..., 0].T, total[..., 0].T], axis=1).reshape(places, rows, 2 * heads_here)
    back_sum, back_stats = [summed[0]], [stats[0]]
    for k in range(1, places):
        pairs = [(p * group + i, ((p - k) % places) * group + i) for p in range(places) for i in range(group)]
        got = lax.ppermute((summed[k], stats[k]), seq, pairs)
        back_sum.append(got[0])
        back_stats.append(got[1])
    summed = jnp.stack(back_sum).astype(jnp.float32).reshape(places, rows, heads_here, HEAD)
    stats = jnp.stack(back_stats)
    top, total = stats[..., :heads_here], stats[..., heads_here:]
    best = jnp.max(top, axis=0)
    factor = jnp.exp(top - best[None])
    total = jnp.sum(total * factor, axis=0)
    summed = jnp.sum(summed * factor[..., None], axis=0)
    attention = (summed / total[..., None]).astype(jnp.bfloat16).reshape(rows, width)
    parts = lax.axis_size("tp")
    terms = jnp.einsum(
        "qf,fkc->kqc", attention, out_weight.reshape(width, parts, -1), preferred_element_type=jnp.float32
    )
    terms = lax.all_to_all(terms.astype(jnp.bfloat16), "tp", split_axis=0, concat_axis=0, tiled=True)
    return jnp.sum(terms.astype(jnp.float32), axis=0).astype(jnp.bfloat16)


def solution(mesh):
    seq_size = mesh.shape["seq"]
    requests = 8
    grid = Mesh(
        np.asarray(mesh.devices).reshape(seq_size // requests, requests, mesh.shape["tp"]),
        ("place", "req", "tp"),
    )
    seq = ("place", "req")
    return jax.shard_map(
        shards,
        mesh=grid,
        in_specs=(
            P(seq, "tp"),
            P(seq, "tp"),
            P(seq, "tp"),
            P(None, seq, "tp"),
            P(None, seq, "tp"),
            P("tp", None),
            P(),
            P(),
            P(),
            P(),
        ),
        out_specs=P(seq, "tp"),
        check_vma=False,
    )
```

```python
import math

import jax
import jax.numpy as jnp
import numpy as np
from jax import lax
from jax.experimental import pallas as pl
from jax.experimental.pallas import tpu as pltpu
from jax.sharding import Mesh
from jax.sharding import PartitionSpec as P

HEAD = 128
GROUP = 4


NEG = -1e30


def attend(q_rows, chunks, params, places, init=None):
    total_rows, width = q_rows.shape
    rows = total_rows // places
    heads = width // HEAD
    n = len(chunks)
    scale = 1.0 / math.sqrt(HEAD)

    def kernel(par, q_ref, *refs):
        kv_refs = refs[:n]
        if init is None:
            o_ref, m_ref, l_ref = refs[n:]
        else:
            a_ref, m0_ref, l0_ref, o_ref, m_ref, l_ref = refs[n:]
        k = pl.program_id(1)
        window = par[2 * n]
        sinks = par[2 * n + 1]
        qpos = par[2 * n + 2 + k] + lax.broadcasted_iota(jnp.int32, (rows, 1), 0)
        q = q_ref[...]
        if init is None:
            m = jnp.full((rows, 1), NEG, jnp.float32)
            l = jnp.zeros((rows, 1), jnp.float32)
            acc = jnp.zeros((rows, HEAD), jnp.float32)
        else:
            m, l, acc = m0_ref[...], l0_ref[...], a_ref[...]
        for c in range(n):
            keys = kv_refs[c][0]
            vals = kv_refs[c][1]
            kpos = par[c] + lax.broadcasted_iota(jnp.int32, (1, keys.shape[0]), 1)
            s = lax.dot_general(q, keys, (((1,), (1,)), ((), ())), preferred_element_type=jnp.float32) * scale
            mask = (kpos <= qpos) & ((qpos - kpos < window) | (kpos < sinks)) & (kpos < par[n + c])
            s = jnp.where(mask, s, NEG)
            m_new = jnp.maximum(m, jnp.max(s, axis=1, keepdims=True))
            alpha = jnp.exp(m - m_new)
            p = jnp.where(mask, jnp.exp(s - m_new), 0.0)
            l = alpha * l + jnp.sum(p, axis=1, keepdims=True)
            acc = alpha * acc + jnp.dot(p.astype(jnp.bfloat16), vals, preferred_element_type=jnp.float32)
            m = m_new
        o_ref[...] = acc
        m_ref[...] = m
        l_ref[...] = l

    row_spec = pl.BlockSpec((rows, HEAD), lambda h, k, par: (k, h))
    stat_spec = pl.BlockSpec((None, rows, 1), lambda h, k, par: (h, k, 0))
    in_specs = [row_spec]
    in_specs += [pl.BlockSpec((2, c.shape[1], HEAD), lambda h, k, par: (0, 0, h)) for c in chunks]
    extra = ()
    if init is not None:
        in_specs += [row_spec, stat_spec, stat_spec]
        extra = tuple(init)
    out_shape = [
        jax.ShapeDtypeStruct((total_rows, width), jnp.float32),
        jax.ShapeDtypeStruct((heads, total_rows, 1), jnp.float32),
        jax.ShapeDtypeStruct((heads, total_rows, 1), jnp.float32),
    ]
    return pl.pallas_call(
        kernel,
        grid_spec=pltpu.PrefetchScalarGridSpec(
            num_scalar_prefetch=1, grid=(heads, places), in_specs=in_specs, out_specs=[row_spec, stat_spec, stat_spec]
        ),
        out_shape=out_shape,
    )(params, q_rows, *chunks, *extra)


def shards(
    query,
    span_keys,
    span_values,
    cache_keys,
    cache_values,
    out_weight,
    cache_lengths,
    sink_counts,
    windows,
    block_of_slot,
):
    rows, width = query.shape
    heads_here = width // HEAD
    places = lax.axis_size("place")
    group = lax.axis_size("req")
    devices = places * group
    place = lax.axis_index("place")
    mine = lax.axis_index("req")
    me = place * group + mine
    cache_dev = cache_keys.shape[1]
    length = cache_lengths[mine]
    window = windows[mine]
    sinks = sink_counts[mine]
    seq = ("place", "req")

    ring = devices // 4
    core, z, y = me % 2, (me // 2) % ring, me // (2 * ring)

    def at(yy, zz, cc):
        return (yy * ring + zz % ring) * 2 + cc

    def request_of(index):
        return index % group

    moves = [(d, flip) for d in (-1, 0, 1) for flip in (0, 1)] + [("far", c) for c in (0, 1)]
    got_kv, got_slot = [], []
    for d, flip in moves:
        if d == "far":
            target = jnp.where(core == 0, at(y, z + 2, flip), at(y, z - 2, 1 - flip))
            source = jnp.where(core == flip, at(y, z - 2, 0), at(y, z + 2, 1))
            pairs = []
            for s_idx in range(devices):
                sc, sz, sy = s_idx % 2, (s_idx // 2) % ring, s_idx // (2 * ring)
                if sc == 0:
                    pairs.append((s_idx, (sy * ring + (sz + 2) % ring) * 2 + flip))
                else:
                    pairs.append((s_idx, (sy * ring + (sz - 2) % ring) * 2 + 1 - flip))
        else:
            target = at(y, z + d, core ^ flip)
            source = at(y, z - d, core ^ flip)
            pairs = []
            for s_idx in range(devices):
                sc, sz, sy = s_idx % 2, (s_idx // 2) % ring, s_idx // (2 * ring)
                pairs.append((s_idx, (sy * ring + (sz + d) % ring) * 2 + (sc ^ flip)))
        sent = request_of(target)
        chunk = jnp.stack(
            [
                lax.dynamic_index_in_dim(cache_keys, sent, 0, keepdims=False),
                lax.dynamic_index_in_dim(cache_values, sent, 0, keepdims=False),
            ]
        )
        if d != 0 or flip != 0:
            chunk = lax.ppermute(chunk, seq, pairs)
        got_kv.append(chunk)
        got_slot.append(source)

    span_q = [query]
    for k in range(1, places):
        pairs = [(p * group + i, ((p + k) % places) * group + i) for p in range(places) for i in range(group)]
        span_q.append(lax.ppermute(query, seq, pairs))
    span_q = jnp.stack(span_q)
    from_place = (place - jnp.arange(places, dtype=jnp.int32)) % places

    slots = jnp.stack(got_slot)
    blocks = block_of_slot[mine][slots]
    first = jnp.concatenate([blocks * cache_dev, jnp.stack([length + place * rows])])
    limits = jnp.concatenate([jnp.broadcast_to(length, (len(got_kv),)), jnp.stack([length + places * rows])])
    tail = jnp.concatenate([jnp.stack([window, sinks]), length + from_place * rows])
    q_all = span_q.reshape(-1, width)
    chunks = got_kv + [jnp.stack([span_keys, span_values])]
    early = [moves.index((0, 0)), moves.index((0, 1)), len(got_kv)]
    late = [c for c in range(len(chunks)) if c not in early]
    state = None
    for part in (early, late):
        picked = jnp.asarray(part, jnp.int32)
        params = jnp.concatenate([first[picked], limits[picked], tail]).astype(jnp.int32)
        state = attend(q_all, [chunks[c] for c in part], params, places, init=state)
    summed, top, total = state
    summed = summed.astype(jnp.bfloat16)
    summed = summed.reshape(places, rows, width)
    stats = jnp.concatenate([top[..., 0].T, total[..., 0].T], axis=1).reshape(places, rows, 2 * heads_here)
    back_sum, back_stats = [summed[0]], [stats[0]]
    for k in range(1, places):
        pairs = [(p * group + i, ((p - k) % places) * group + i) for p in range(places) for i in range(group)]
        got = lax.ppermute((summed[k], stats[k]), seq, pairs)
        back_sum.append(got[0])
        back_stats.append(got[1])
    summed = jnp.stack(back_sum).astype(jnp.float32).reshape(places, rows, heads_here, HEAD)
    stats = jnp.stack(back_stats)
    top, total = stats[..., :heads_here], stats[..., heads_here:]
    best = jnp.max(top, axis=0)
    factor = jnp.exp(top - best[None])
    total = jnp.sum(total * factor, axis=0)
    summed = jnp.sum(summed * factor[..., None], axis=0)
    attention = (summed / total[..., None]).astype(jnp.bfloat16).reshape(rows, width)
    parts = lax.axis_size("tp")
    terms = jnp.einsum(
        "qf,fkc->kqc", attention, out_weight.reshape(width, parts, -1), preferred_element_type=jnp.float32
    )
    terms = lax.all_to_all(terms.astype(jnp.bfloat16), "tp", split_axis=0, concat_axis=0, tiled=True)
    return jnp.sum(terms.astype(jnp.float32), axis=0).astype(jnp.bfloat16)


def solution(mesh):
    seq_size = mesh.shape["seq"]
    requests = 8
    grid = Mesh(
        np.asarray(mesh.devices).reshape(seq_size // requests, requests, mesh.shape["tp"]),
        ("place", "req", "tp"),
    )
    seq = ("place", "req")
    return jax.shard_map(
        shards,
        mesh=grid,
        in_specs=(
            P(seq, "tp"),
            P(seq, "tp"),
            P(seq, "tp"),
            P(None, seq, "tp"),
            P(None, seq, "tp"),
            P("tp", None),
            P(),
            P(),
            P(),
            P(),
        ),
        out_specs=P(seq, "tp"),
        check_vma=False,
    )
```

```python
import math

import jax
import jax.numpy as jnp
import numpy as np
from jax import lax
from jax.experimental import pallas as pl
from jax.experimental.pallas import tpu as pltpu
from jax.sharding import Mesh
from jax.sharding import PartitionSpec as P

HEAD = 128
GROUP = 4


NEG = -1e30


def attend(q_rows, chunks, span_k, span_v, params, places, interpret=False):
    total_rows, width = q_rows.shape
    rows = total_rows // places
    heads = width // HEAD
    n = len(chunks)
    cdev = chunks[0].shape[1]
    srows = span_k.shape[0]
    scale = 1.0 / math.sqrt(HEAD)

    def kernel(par, q_ref, *refs):
        kv_refs = refs[:n]
        sk_ref, sv_ref, o_ref, m_ref, l_ref, m_s, l_s, a_s = refs[n:]
        k = pl.program_id(1)
        length = par[n + 1]
        window = par[n + 2]
        sinks = par[n + 3]
        first_q = par[n + 4 + k]
        qpos = first_q + lax.broadcasted_iota(jnp.int32, (rows, 1), 0)
        q = q_ref[...]
        m_s[...] = jnp.full((rows, 1), NEG, jnp.float32)
        l_s[...] = jnp.zeros((rows, 1), jnp.float32)
        a_s[...] = jnp.zeros((rows, HEAD), jnp.float32)
        for c in range(n + 1):
            if c < n:
                base, size, limit = par[c], cdev, length
            else:
                base, size, limit = par[n], srows, length + total_rows
            unseen = (
                (base >= limit)
                | (base > first_q + rows - 1)
                | ((base >= sinks) & (first_q - (base + size - 1) >= window))
            )

            @pl.when(jnp.logical_not(unseen))
            def _(c=c, base=base, size=size, limit=limit):
                if c < n:
                    keys = kv_refs[c][0]
                    vals = kv_refs[c][1]
                else:
                    keys = sk_ref[...]
                    vals = sv_ref[...]
                kpos = base + lax.broadcasted_iota(jnp.int32, (1, size), 1)
                s = lax.dot_general(q, keys, (((1,), (1,)), ((), ())), preferred_element_type=jnp.float32) * scale
                mask = (kpos <= qpos) & ((qpos - kpos < window) | (kpos < sinks)) & (kpos < limit)
                s = jnp.where(mask, s, NEG)
                m = m_s[...]
                m_new = jnp.maximum(m, jnp.max(s, axis=1, keepdims=True))
                alpha = jnp.exp(m - m_new)
                p = jnp.exp(s - jnp.where(m_new > NEG, m_new, 0.0))
                l_s[...] = alpha * l_s[...] + jnp.sum(p, axis=1, keepdims=True)
                a_s[...] = alpha * a_s[...] + jnp.dot(
                    p.astype(jnp.bfloat16), vals, preferred_element_type=jnp.float32
                )
                m_s[...] = m_new

        o_ref[...] = a_s[...].astype(o_ref.dtype)
        m_ref[...] = m_s[...]
        l_ref[...] = l_s[...]

    in_specs = [pl.BlockSpec((rows, HEAD), lambda h, k, par: (k, h))]
    in_specs += [pl.BlockSpec((2, cdev, HEAD), lambda h, k, par: (0, 0, h)) for _ in range(n)]
    in_specs += [pl.BlockSpec((srows, HEAD), lambda h, k, par: (0, h))] * 2
    out_specs = [
        pl.BlockSpec((rows, HEAD), lambda h, k, par: (k, h)),
        pl.BlockSpec((None, rows, 1), lambda h, k, par: (h, k, 0)),
        pl.BlockSpec((None, rows, 1), lambda h, k, par: (h, k, 0)),
    ]
    out_shape = [
        jax.ShapeDtypeStruct((total_rows, width), jnp.bfloat16),
        jax.ShapeDtypeStruct((heads, total_rows, 1), jnp.float32),
        jax.ShapeDtypeStruct((heads, total_rows, 1), jnp.float32),
    ]
    return pl.pallas_call(
        kernel,
        grid_spec=pltpu.PrefetchScalarGridSpec(
            num_scalar_prefetch=1,
            grid=(heads, places),
            in_specs=in_specs,
            out_specs=out_specs,
            scratch_shapes=[
                pltpu.VMEM((rows, 1), jnp.float32),
                pltpu.VMEM((rows, 1), jnp.float32),
                pltpu.VMEM((rows, HEAD), jnp.float32),
            ],
        ),
        out_shape=out_shape,
        interpret=interpret,
    )(params, q_rows, *chunks, span_k, span_v)


def shards(
    query,
    span_keys,
    span_values,
    cache_keys,
    cache_values,
    out_weight,
    cache_lengths,
    sink_counts,
    windows,
    block_of_slot,
):
    rows, width = query.shape
    heads_here = width // HEAD
    places = lax.axis_size("place")
    group = lax.axis_size("req")
    devices = places * group
    place = lax.axis_index("place")
    mine = lax.axis_index("req")
    me = place * group + mine
    cache_dev = cache_keys.shape[1]
    length = cache_lengths[mine]
    window = windows[mine]
    sinks = sink_counts[mine]
    seq = ("place", "req")

    ring = devices // 4
    core, z, y = me % 2, (me // 2) % ring, me // (2 * ring)

    def at(yy, zz, cc):
        return (yy * ring + zz % ring) * 2 + cc

    def request_of(index):
        return index % group

    moves = [(d, flip) for d in (-1, 0, 1) for flip in (0, 1)] + [("far", c) for c in (0, 1)]
    got_kv, got_slot = [], []
    for d, flip in moves:
        if d == "far":
            target = jnp.where(core == 0, at(y, z + 2, flip), at(y, z - 2, 1 - flip))
            source = jnp.where(core == flip, at(y, z - 2, 0), at(y, z + 2, 1))
            pairs = []
            for s_idx in range(devices):
                sc, sz, sy = s_idx % 2, (s_idx // 2) % ring, s_idx // (2 * ring)
                if sc == 0:
                    pairs.append((s_idx, (sy * ring + (sz + 2) % ring) * 2 + flip))
                else:
                    pairs.append((s_idx, (sy * ring + (sz - 2) % ring) * 2 + 1 - flip))
        else:
            target = at(y, z + d, core ^ flip)
            source = at(y, z - d, core ^ flip)
            pairs = []
            for s_idx in range(devices):
                sc, sz, sy = s_idx % 2, (s_idx // 2) % ring, s_idx // (2 * ring)
                pairs.append((s_idx, (sy * ring + (sz + d) % ring) * 2 + (sc ^ flip)))
        sent = request_of(target)
        chunk = jnp.stack(
            [
                lax.dynamic_index_in_dim(cache_keys, sent, 0, keepdims=False),
                lax.dynamic_index_in_dim(cache_values, sent, 0, keepdims=False),
            ]
        )
        if d != 0 or flip != 0:
            chunk = lax.ppermute(chunk, seq, pairs)
        got_kv.append(chunk)
        got_slot.append(source)

    span_q = [query]
    for k in range(1, places):
        pairs = [(p * group + i, ((p + k) % places) * group + i) for p in range(places) for i in range(group)]
        span_q.append(lax.ppermute(query, seq, pairs))
    span_q = jnp.stack(span_q)
    from_place = (place - jnp.arange(places, dtype=jnp.int32)) % places

    slots = jnp.stack(got_slot)
    blocks = block_of_slot[mine][slots]
    params = jnp.concatenate(
        [
            blocks * cache_dev,
            jnp.stack([length + place * rows, length, window, sinks]),
            length + from_place * rows,
        ]
    ).astype(jnp.int32)
    summed, top, total = attend(span_q.reshape(-1, width), got_kv, span_keys, span_values, params, places)
    summed = summed.reshape(places, rows, width)
    stats = jnp.concatenate([top[..., 0].T, total[..., 0].T], axis=1).reshape(places, rows, 2 * heads_here)
    back_sum, back_stats = [summed[0]], [stats[0]]
    for k in range(1, places):
        pairs = [(p * group + i, ((p - k) % places) * group + i) for p in range(places) for i in range(group)]
        got = lax.ppermute((summed[k], stats[k]), seq, pairs)
        back_sum.append(got[0])
        back_stats.append(got[1])
    summed = jnp.stack(back_sum).astype(jnp.float32).reshape(places, rows, heads_here, HEAD)
    stats = jnp.stack(back_stats)
    top, total = stats[..., :heads_here], stats[..., heads_here:]
    best = jnp.max(top, axis=0)
    factor = jnp.exp(top - best[None])
    total = jnp.sum(total * factor, axis=0)
    summed = jnp.sum(summed * factor[..., None], axis=0)
    attention = (summed / total[..., None]).astype(jnp.bfloat16).reshape(rows, width)
    parts = lax.axis_size("tp")
    terms = jnp.einsum(
        "qf,fkc->kqc", attention, out_weight.reshape(width, parts, -1), preferred_element_type=jnp.float32
    )
    terms = lax.all_to_all(terms.astype(jnp.bfloat16), "tp", split_axis=0, concat_axis=0, tiled=True)
    return jnp.sum(terms.astype(jnp.float32), axis=0).astype(jnp.bfloat16)


def solution(mesh):
    seq_size = mesh.shape["seq"]
    requests = 8
    grid = Mesh(
        np.asarray(mesh.devices).reshape(seq_size // requests, requests, mesh.shape["tp"]),
        ("place", "req", "tp"),
    )
    seq = ("place", "req")
    return jax.shard_map(
        shards,
        mesh=grid,
        in_specs=(
            P(seq, "tp"),
            P(seq, "tp"),
            P(seq, "tp"),
            P(None, seq, "tp"),
            P(None, seq, "tp"),
            P("tp", None),
            P(),
            P(),
            P(),
            P(),
        ),
        out_specs=P(seq, "tp"),
        check_vma=False,
    )
```

```python
import math

import jax
import jax.numpy as jnp
import numpy as np
from jax import lax
from jax.experimental import pallas as pl
from jax.experimental.pallas import tpu as pltpu
from jax.sharding import Mesh
from jax.sharding import PartitionSpec as P

HEAD = 128
GROUP = 4


NEG = -1e30


def attend(q_rows, chunks, span_k, span_v, params, places, interpret=False):
    total_rows, width = q_rows.shape
    rows = total_rows // places
    heads = width // HEAD
    n = len(chunks)
    cdev = chunks[0].shape[1]
    srows = span_k.shape[0]
    scale = 1.0 / math.sqrt(HEAD)

    def kernel(par, q_ref, *refs):
        kv_refs = refs[:n]
        sk_ref, sv_ref, o_ref, m_ref, l_ref = refs[n:]
        k = pl.program_id(1)
        length = par[n + 1]
        window = par[n + 2]
        sinks = par[n + 3]
        qpos = par[n + 4 + k] + lax.broadcasted_iota(jnp.int32, (rows, 1), 0)
        q = q_ref[...]
        m = jnp.full((rows, 1), NEG, jnp.float32)
        l = jnp.zeros((rows, 1), jnp.float32)
        acc = jnp.zeros((rows, HEAD), jnp.float32)
        for c in range(n + 1):
            if c < n:
                keys = kv_refs[c][0]
                vals = kv_refs[c][1]
                kpos = par[c] + lax.broadcasted_iota(jnp.int32, (1, cdev), 1)
                valid = kpos < length
            else:
                keys = sk_ref[...]
                vals = sv_ref[...]
                kpos = par[n] + lax.broadcasted_iota(jnp.int32, (1, srows), 1)
                valid = kpos >= 0
            s = lax.dot_general(q, keys, (((1,), (1,)), ((), ())), preferred_element_type=jnp.float32) * scale
            mask = (kpos <= qpos) & ((qpos - kpos < window) | (kpos < sinks)) & valid
            s = jnp.where(mask, s, NEG)
            m_new = jnp.maximum(m, jnp.max(s, axis=1, keepdims=True))
            alpha = jnp.exp(m - m_new)
            p = jnp.exp(s - jnp.where(m_new > NEG, m_new, 0.0))
            l = alpha * l + jnp.sum(p, axis=1, keepdims=True)
            acc = alpha * acc + jnp.dot(p.astype(jnp.bfloat16), vals, preferred_element_type=jnp.float32)
            m = m_new
        o_ref[...] = acc.astype(o_ref.dtype)
        m_ref[...] = m
        l_ref[...] = l

    in_specs = [pl.BlockSpec((rows, HEAD), lambda h, k, par: (k, h))]
    in_specs += [pl.BlockSpec((2, cdev, HEAD), lambda h, k, par: (0, 0, h)) for _ in range(n)]
    in_specs += [pl.BlockSpec((srows, HEAD), lambda h, k, par: (0, h))] * 2
    out_specs = [
        pl.BlockSpec((rows, HEAD), lambda h, k, par: (k, h)),
        pl.BlockSpec((None, rows, 1), lambda h, k, par: (h, k, 0)),
        pl.BlockSpec((None, rows, 1), lambda h, k, par: (h, k, 0)),
    ]
    out_shape = [
        jax.ShapeDtypeStruct((total_rows, width), jnp.bfloat16),
        jax.ShapeDtypeStruct((heads, total_rows, 1), jnp.float32),
        jax.ShapeDtypeStruct((heads, total_rows, 1), jnp.float32),
    ]
    return pl.pallas_call(
        kernel,
        grid_spec=pltpu.PrefetchScalarGridSpec(
            num_scalar_prefetch=1, grid=(heads, places), in_specs=in_specs, out_specs=out_specs
        ),
        out_shape=out_shape,
        interpret=interpret,
    )(params, q_rows, *chunks, span_k, span_v)


def shards(
    query,
    span_keys,
    span_values,
    cache_keys,
    cache_values,
    out_weight,
    cache_lengths,
    sink_counts,
    windows,
    block_of_slot,
):
    rows, width = query.shape
    heads_here = width // HEAD
    places = lax.axis_size("place")
    group = lax.axis_size("req")
    devices = places * group
    place = lax.axis_index("place")
    mine = lax.axis_index("req")
    me = place * group + mine
    cache_dev = cache_keys.shape[1]
    length = cache_lengths[mine]
    window = windows[mine]
    sinks = sink_counts[mine]
    seq = ("place", "req")

    ring = devices // 4
    core, z, y = me % 2, (me // 2) % ring, me // (2 * ring)

    def at(yy, zz, cc):
        return (yy * ring + zz % ring) * 2 + cc

    def request_of(index):
        return index % group

    moves = [(d, flip) for d in (-1, 0, 1) for flip in (0, 1)] + [("far", c) for c in (0, 1)]
    got_kv, got_slot = [], []
    for d, flip in moves:
        if d == "far":
            target = jnp.where(core == 0, at(y, z + 2, flip), at(y, z - 2, 1 - flip))
            source = jnp.where(core == flip, at(y, z - 2, 0), at(y, z + 2, 1))
            pairs = []
            for s_idx in range(devices):
                sc, sz, sy = s_idx % 2, (s_idx // 2) % ring, s_idx // (2 * ring)
                if sc == 0:
                    pairs.append((s_idx, (sy * ring + (sz + 2) % ring) * 2 + flip))
                else:
                    pairs.append((s_idx, (sy * ring + (sz - 2) % ring) * 2 + 1 - flip))
        else:
            target = at(y, z + d, core ^ flip)
            source = at(y, z - d, core ^ flip)
            pairs = []
            for s_idx in range(devices):
                sc, sz, sy = s_idx % 2, (s_idx // 2) % ring, s_idx // (2 * ring)
                pairs.append((s_idx, (sy * ring + (sz + d) % ring) * 2 + (sc ^ flip)))
        sent = request_of(target)
        chunk = jnp.stack(
            [
                lax.dynamic_index_in_dim(cache_keys, sent, 0, keepdims=False),
                lax.dynamic_index_in_dim(cache_values, sent, 0, keepdims=False),
            ]
        )
        if d != 0 or flip != 0:
            chunk = lax.ppermute(chunk, seq, pairs)
        got_kv.append(chunk)
        got_slot.append(source)

    span_q = [query]
    for k in range(1, places):
        pairs = [(p * group + i, ((p + k) % places) * group + i) for p in range(places) for i in range(group)]
        span_q.append(lax.ppermute(query, seq, pairs))
    span_q = jnp.stack(span_q)
    from_place = (place - jnp.arange(places, dtype=jnp.int32)) % places

    slots = jnp.stack(got_slot)
    blocks = block_of_slot[mine][slots]
    params = jnp.concatenate(
        [
            blocks * cache_dev,
            jnp.stack([length + place * rows, length, window, sinks]),
            length + from_place * rows,
        ]
    ).astype(jnp.int32)
    summed, top, total = attend(span_q.reshape(-1, width), got_kv, span_keys, span_values, params, places)
    summed = summed.reshape(places, rows, width)
    stats = jnp.concatenate([top[..., 0].T, total[..., 0].T], axis=1).reshape(places, rows, 2 * heads_here)
    back_sum, back_stats = [summed[0]], [stats[0]]
    for k in range(1, places):
        pairs = [(p * group + i, ((p - k) % places) * group + i) for p in range(places) for i in range(group)]
        got = lax.ppermute((summed[k], stats[k]), seq, pairs)
        back_sum.append(got[0])
        back_stats.append(got[1])
    summed = jnp.stack(back_sum).astype(jnp.float32).reshape(places, rows, heads_here, HEAD)
    stats = jnp.stack(back_stats)
    top, total = stats[..., :heads_here], stats[..., heads_here:]
    best = jnp.max(top, axis=0)
    factor = jnp.exp(top - best[None])
    total = jnp.sum(total * factor, axis=0)
    summed = jnp.sum(summed * factor[..., None], axis=0)
    attention = (summed / total[..., None]).astype(jnp.bfloat16).reshape(rows, width)
    parts = lax.axis_size("tp")
    terms = jnp.einsum(
        "qf,fkc->kqc", attention, out_weight.reshape(width, parts, -1), preferred_element_type=jnp.float32
    )
    terms = lax.all_to_all(terms.astype(jnp.bfloat16), "tp", split_axis=0, concat_axis=0, tiled=True)
    return jnp.sum(terms.astype(jnp.float32), axis=0).astype(jnp.bfloat16)


def solution(mesh):
    seq_size = mesh.shape["seq"]
    requests = 8
    grid = Mesh(
        np.asarray(mesh.devices).reshape(seq_size // requests, requests, mesh.shape["tp"]),
        ("place", "req", "tp"),
    )
    seq = ("place", "req")
    return jax.shard_map(
        shards,
        mesh=grid,
        in_specs=(
            P(seq, "tp"),
            P(seq, "tp"),
            P(seq, "tp"),
            P(None, seq, "tp"),
            P(None, seq, "tp"),
            P("tp", None),
            P(),
            P(),
            P(),
            P(),
        ),
        out_specs=P(seq, "tp"),
        check_vma=False,
    )
```

```python
import math

import jax
import jax.numpy as jnp
import numpy as np
from jax import lax
from jax.experimental import pallas as pl
from jax.experimental.pallas import tpu as pltpu
from jax.sharding import Mesh
from jax.sharding import PartitionSpec as P

HEAD = 128
GROUP = 4


NEG = -1e30


def attend(q_rows, chunks, span_k, span_v, params, places, interpret=False):
    total_rows, width = q_rows.shape
    rows = total_rows // places
    heads = width // HEAD
    n = len(chunks)
    cdev = chunks[0].shape[1]
    srows = span_k.shape[0]
    scale = 1.0 / math.sqrt(HEAD)

    def kernel(par, q_ref, *refs):
        kv_refs = refs[:n]
        sk_ref, sv_ref, o_ref, m_ref, l_ref = refs[n:]
        length = par[n + 1]
        window = par[n + 2]
        sinks = par[n + 3]
        row = lax.broadcasted_iota(jnp.int32, (total_rows, 1), 0)
        qpos = row % rows
        for j in range(places):
            qpos = jnp.where(row // rows == j, qpos + par[n + 4 + j], qpos)
        rows_here = total_rows
        q = q_ref[...]
        m = jnp.full((rows_here, 1), NEG, jnp.float32)
        l = jnp.zeros((rows_here, 1), jnp.float32)
        acc = jnp.zeros((rows_here, HEAD), jnp.float32)
        for c in range(n + 1):
            if c < n:
                keys = kv_refs[c][0]
                vals = kv_refs[c][1]
                kpos = par[c] + lax.broadcasted_iota(jnp.int32, (1, cdev), 1)
                valid = kpos < length
            else:
                keys = sk_ref[...]
                vals = sv_ref[...]
                kpos = par[n] + lax.broadcasted_iota(jnp.int32, (1, srows), 1)
                valid = kpos >= 0
            s = lax.dot_general(q, keys, (((1,), (1,)), ((), ())), preferred_element_type=jnp.float32) * scale
            mask = (kpos <= qpos) & ((qpos - kpos < window) | (kpos < sinks)) & valid
            s = jnp.where(mask, s, NEG)
            m_new = jnp.maximum(m, jnp.max(s, axis=1, keepdims=True))
            alpha = jnp.exp(m - m_new)
            p = jnp.exp(s - jnp.where(m_new > NEG, m_new, 0.0))
            l = alpha * l + jnp.sum(p, axis=1, keepdims=True)
            acc = alpha * acc + jnp.dot(p.astype(jnp.bfloat16), vals, preferred_element_type=jnp.float32)
            m = m_new
        o_ref[...] = acc.astype(o_ref.dtype)
        m_ref[...] = m
        l_ref[...] = l

    in_specs = [pl.BlockSpec((total_rows, HEAD), lambda h, par: (0, h))]
    in_specs += [pl.BlockSpec((2, cdev, HEAD), lambda h, par: (0, 0, h)) for _ in range(n)]
    in_specs += [pl.BlockSpec((srows, HEAD), lambda h, par: (0, h))] * 2
    out_specs = [
        pl.BlockSpec((total_rows, HEAD), lambda h, par: (0, h)),
        pl.BlockSpec((None, total_rows, 1), lambda h, par: (h, 0, 0)),
        pl.BlockSpec((None, total_rows, 1), lambda h, par: (h, 0, 0)),
    ]
    out_shape = [
        jax.ShapeDtypeStruct((total_rows, width), jnp.bfloat16),
        jax.ShapeDtypeStruct((heads, total_rows, 1), jnp.float32),
        jax.ShapeDtypeStruct((heads, total_rows, 1), jnp.float32),
    ]
    return pl.pallas_call(
        kernel,
        grid_spec=pltpu.PrefetchScalarGridSpec(
            num_scalar_prefetch=1, grid=(heads,), in_specs=in_specs, out_specs=out_specs
        ),
        out_shape=out_shape,
        interpret=interpret,
    )(params, q_rows, *chunks, span_k, span_v)


def shards(
    query,
    span_keys,
    span_values,
    cache_keys,
    cache_values,
    out_weight,
    cache_lengths,
    sink_counts,
    windows,
    block_of_slot,
):
    rows, width = query.shape
    heads_here = width // HEAD
    places = lax.axis_size("place")
    group = lax.axis_size("req")
    devices = places * group
    place = lax.axis_index("place")
    mine = lax.axis_index("req")
    me = place * group + mine
    cache_dev = cache_keys.shape[1]
    length = cache_lengths[mine]
    window = windows[mine]
    sinks = sink_counts[mine]
    seq = ("place", "req")

    ring = devices // 4
    core, z, y = me % 2, (me // 2) % ring, me // (2 * ring)

    def at(yy, zz, cc):
        return (yy * ring + zz % ring) * 2 + cc

    def request_of(index):
        return index % group

    moves = [(d, flip) for d in (-1, 0, 1) for flip in (0, 1)] + [("far", c) for c in (0, 1)]
    got_kv, got_slot = [], []
    for d, flip in moves:
        if d == "far":
            target = jnp.where(core == 0, at(y, z + 2, flip), at(y, z - 2, 1 - flip))
            source = jnp.where(core == flip, at(y, z - 2, 0), at(y, z + 2, 1))
            pairs = []
            for s_idx in range(devices):
                sc, sz, sy = s_idx % 2, (s_idx // 2) % ring, s_idx // (2 * ring)
                if sc == 0:
                    pairs.append((s_idx, (sy * ring + (sz + 2) % ring) * 2 + flip))
                else:
                    pairs.append((s_idx, (sy * ring + (sz - 2) % ring) * 2 + 1 - flip))
        else:
            target = at(y, z + d, core ^ flip)
            source = at(y, z - d, core ^ flip)
            pairs = []
            for s_idx in range(devices):
                sc, sz, sy = s_idx % 2, (s_idx // 2) % ring, s_idx // (2 * ring)
                pairs.append((s_idx, (sy * ring + (sz + d) % ring) * 2 + (sc ^ flip)))
        sent = request_of(target)
        chunk = jnp.stack(
            [
                lax.dynamic_index_in_dim(cache_keys, sent, 0, keepdims=False),
                lax.dynamic_index_in_dim(cache_values, sent, 0, keepdims=False),
            ]
        )
        if d != 0 or flip != 0:
            chunk = lax.ppermute(chunk, seq, pairs)
        got_kv.append(chunk)
        got_slot.append(source)

    span_q = [query]
    for k in range(1, places):
        pairs = [(p * group + i, ((p + k) % places) * group + i) for p in range(places) for i in range(group)]
        span_q.append(lax.ppermute(query, seq, pairs))
    span_q = jnp.stack(span_q)
    from_place = (place - jnp.arange(places, dtype=jnp.int32)) % places

    slots = jnp.stack(got_slot)
    blocks = block_of_slot[mine][slots]
    params = jnp.concatenate(
        [
            blocks * cache_dev,
            jnp.stack([length + place * rows, length, window, sinks]),
            length + from_place * rows,
        ]
    ).astype(jnp.int32)
    summed, top, total = attend(span_q.reshape(-1, width), got_kv, span_keys, span_values, params, places)
    summed = summed.reshape(places, rows, width)
    stats = jnp.concatenate([top[..., 0].T, total[..., 0].T], axis=1).reshape(places, rows, 2 * heads_here)
    back_sum, back_stats = [summed[0]], [stats[0]]
    for k in range(1, places):
        pairs = [(p * group + i, ((p - k) % places) * group + i) for p in range(places) for i in range(group)]
        got = lax.ppermute((summed[k], stats[k]), seq, pairs)
        back_sum.append(got[0])
        back_stats.append(got[1])
    summed = jnp.stack(back_sum).astype(jnp.float32).reshape(places, rows, heads_here, HEAD)
    stats = jnp.stack(back_stats)
    top, total = stats[..., :heads_here], stats[..., heads_here:]
    best = jnp.max(top, axis=0)
    factor = jnp.exp(top - best[None])
    total = jnp.sum(total * factor, axis=0)
    summed = jnp.sum(summed * factor[..., None], axis=0)
    attention = (summed / total[..., None]).astype(jnp.bfloat16).reshape(rows, width)
    parts = lax.axis_size("tp")
    terms = jnp.einsum(
        "qf,fkc->kqc", attention, out_weight.reshape(width, parts, -1), preferred_element_type=jnp.float32
    )
    terms = lax.all_to_all(terms.astype(jnp.bfloat16), "tp", split_axis=0, concat_axis=0, tiled=True)
    return jnp.sum(terms.astype(jnp.float32), axis=0).astype(jnp.bfloat16)


def solution(mesh):
    seq_size = mesh.shape["seq"]
    requests = 8
    grid = Mesh(
        np.asarray(mesh.devices).reshape(seq_size // requests, requests, mesh.shape["tp"]),
        ("place", "req", "tp"),
    )
    seq = ("place", "req")
    return jax.shard_map(
        shards,
        mesh=grid,
        in_specs=(
            P(seq, "tp"),
            P(seq, "tp"),
            P(seq, "tp"),
            P(None, seq, "tp"),
            P(None, seq, "tp"),
            P("tp", None),
            P(),
            P(),
            P(),
            P(),
        ),
        out_specs=P(seq, "tp"),
        check_vma=False,
    )
```

```python
import math

import jax
import jax.numpy as jnp
import numpy as np
from jax import lax
from jax.experimental import pallas as pl
from jax.experimental.pallas import tpu as pltpu
from jax.sharding import Mesh
from jax.sharding import PartitionSpec as P

HEAD = 128


NEG = -1e30


def attend(q_rows, chunks, span_k, span_v, params, places, interpret=False):
    total_rows, width = q_rows.shape
    rows = total_rows // places
    heads = width // HEAD
    n = len(chunks)
    cdev = chunks[0].shape[1]
    srows = span_k.shape[0]
    scale = 1.0 / math.sqrt(HEAD)

    def kernel(par, q_ref, *refs):
        kv_refs = refs[:n]
        sk_ref, sv_ref, o_ref, m_ref, l_ref = refs[n:]
        length = par[n + 1]
        window = par[n + 2]
        sinks = par[n + 3]
        row = lax.broadcasted_iota(jnp.int32, (total_rows, 1), 0)
        qpos = row % rows
        for j in range(places):
            qpos = jnp.where(row // rows == j, qpos + par[n + 4 + j], qpos)
        rows_here = total_rows
        q = q_ref[...]
        m = jnp.full((rows_here, 1), NEG, jnp.float32)
        l = jnp.zeros((rows_here, 1), jnp.float32)
        acc = jnp.zeros((rows_here, HEAD), jnp.float32)
        for c in range(n + 1):
            if c < n:
                keys = kv_refs[c][0]
                vals = kv_refs[c][1]
                kpos = par[c] + lax.broadcasted_iota(jnp.int32, (1, cdev), 1)
                valid = kpos < length
            else:
                keys = sk_ref[...]
                vals = sv_ref[...]
                kpos = par[n] + lax.broadcasted_iota(jnp.int32, (1, srows), 1)
                valid = kpos >= 0
            s = lax.dot_general(q, keys, (((1,), (1,)), ((), ())), preferred_element_type=jnp.float32) * scale
            mask = (kpos <= qpos) & ((qpos - kpos < window) | (kpos < sinks)) & valid
            s = jnp.where(mask, s, NEG)
            m_new = jnp.maximum(m, jnp.max(s, axis=1, keepdims=True))
            alpha = jnp.exp(m - m_new)
            p = jnp.exp(s - jnp.where(m_new > NEG, m_new, 0.0))
            l = alpha * l + jnp.sum(p, axis=1, keepdims=True)
            acc = alpha * acc + jnp.dot(p.astype(jnp.bfloat16), vals, preferred_element_type=jnp.float32)
            m = m_new
        o_ref[...] = acc.astype(o_ref.dtype)
        m_ref[...] = m
        l_ref[...] = l

    in_specs = [pl.BlockSpec((total_rows, HEAD), lambda h, par: (0, h))]
    in_specs += [pl.BlockSpec((2, cdev, HEAD), lambda h, par: (0, 0, h)) for _ in range(n)]
    in_specs += [pl.BlockSpec((srows, HEAD), lambda h, par: (0, h))] * 2
    out_specs = [
        pl.BlockSpec((total_rows, HEAD), lambda h, par: (0, h)),
        pl.BlockSpec((None, total_rows, 1), lambda h, par: (h, 0, 0)),
        pl.BlockSpec((None, total_rows, 1), lambda h, par: (h, 0, 0)),
    ]
    out_shape = [
        jax.ShapeDtypeStruct((total_rows, width), jnp.bfloat16),
        jax.ShapeDtypeStruct((heads, total_rows, 1), jnp.float32),
        jax.ShapeDtypeStruct((heads, total_rows, 1), jnp.float32),
    ]
    return pl.pallas_call(
        kernel,
        grid_spec=pltpu.PrefetchScalarGridSpec(
            num_scalar_prefetch=1, grid=(heads,), in_specs=in_specs, out_specs=out_specs
        ),
        out_shape=out_shape,
        interpret=interpret,
    )(params, q_rows, *chunks, span_k, span_v)


def layer(
    query,
    span_keys,
    span_values,
    cache_keys,
    cache_values,
    out_weight,
    cache_lengths,
    sink_counts,
    windows,
    block_of_slot,
):
    rows, width = query.shape
    heads_here = width // HEAD
    places = lax.axis_size("place")
    group = lax.axis_size("req")
    devices = places * group
    place = lax.axis_index("place")
    mine = lax.axis_index("req")
    me = place * group + mine
    cache_dev = cache_keys.shape[1]
    length = cache_lengths[mine]
    window = windows[mine]
    sinks = sink_counts[mine]
    seq = ("place", "req")

    ring = devices // 4
    core, z, y = me % 2, (me // 2) % ring, me // (2 * ring)

    def at(yy, zz, cc):
        return (yy * ring + zz % ring) * 2 + cc

    def request_of(index):
        return index % group

    moves = [(d, flip) for d in (-1, 0, 1) for flip in (0, 1)] + [("far", c) for c in (0, 1)]
    got_kv, got_slot = [], []
    for d, flip in moves:
        if d == "far":
            target = jnp.where(core == 0, at(y, z + 2, flip), at(y, z - 2, 1 - flip))
            source = jnp.where(core == flip, at(y, z - 2, 0), at(y, z + 2, 1))
            pairs = []
            for s_idx in range(devices):
                sc, sz, sy = s_idx % 2, (s_idx // 2) % ring, s_idx // (2 * ring)
                if sc == 0:
                    pairs.append((s_idx, (sy * ring + (sz + 2) % ring) * 2 + flip))
                else:
                    pairs.append((s_idx, (sy * ring + (sz - 2) % ring) * 2 + 1 - flip))
        else:
            target = at(y, z + d, core ^ flip)
            source = at(y, z - d, core ^ flip)
            pairs = []
            for s_idx in range(devices):
                sc, sz, sy = s_idx % 2, (s_idx // 2) % ring, s_idx // (2 * ring)
                pairs.append((s_idx, (sy * ring + (sz + d) % ring) * 2 + (sc ^ flip)))
        sent = request_of(target)
        chunk = jnp.stack(
            [
                lax.dynamic_index_in_dim(cache_keys, sent, 0, keepdims=False),
                lax.dynamic_index_in_dim(cache_values, sent, 0, keepdims=False),
            ]
        )
        if d != 0 or flip != 0:
            chunk = lax.ppermute(chunk, seq, pairs)
        got_kv.append(chunk)
        got_slot.append(source)

    span_q = [query]
    for k in range(1, places):
        pairs = [(p * group + i, ((p + k) % places) * group + i) for p in range(places) for i in range(group)]
        span_q.append(lax.ppermute(query, seq, pairs))
    span_q = jnp.stack(span_q)
    from_place = (place - jnp.arange(places, dtype=jnp.int32)) % places

    slots = jnp.stack(got_slot)
    blocks = block_of_slot[mine][slots]
    head_params = jnp.concatenate(
        [blocks * cache_dev, jnp.stack([length + place * rows, length, window, sinks])]
    )
    first_rows = length + from_place * rows

    def partial(picked):
        params = jnp.concatenate([head_params, first_rows[picked[0] : picked[-1] + 1]]).astype(jnp.int32)
        q_rows = span_q[picked[0] : picked[-1] + 1].reshape(-1, width)
        out, top, total = attend(q_rows, got_kv, span_keys, span_values, params, len(picked))
        stats = jnp.concatenate([top[..., 0].T, total[..., 0].T], axis=1)
        return out.reshape(len(picked), rows, width), stats.reshape(len(picked), rows, 2 * heads_here)

    other_sum, other_stats = partial(list(range(1, places)))
    own_sum, own_stats = partial([0])
    back_sum, back_stats = [own_sum[0]], [own_stats[0]]
    for k in range(1, places):
        pairs = [(p * group + i, ((p - k) % places) * group + i) for p in range(places) for i in range(group)]
        got = lax.ppermute((other_sum[k - 1], other_stats[k - 1]), seq, pairs)
        back_sum.append(got[0])
        back_stats.append(got[1])
    summed = jnp.stack(back_sum).astype(jnp.float32).reshape(places, rows, heads_here, HEAD)
    stats = jnp.stack(back_stats)
    top, total = stats[..., :heads_here], stats[..., heads_here:]
    best = jnp.max(top, axis=0)
    factor = jnp.exp(top - best[None])
    total = jnp.sum(total * factor, axis=0)
    summed = jnp.sum(summed * factor[..., None], axis=0)
    attention = (summed / total[..., None]).astype(jnp.bfloat16).reshape(rows, width)
    parts = lax.axis_size("tp")
    terms = jnp.einsum(
        "qf,fkc->kqc", attention, out_weight.reshape(width, parts, -1), preferred_element_type=jnp.float32
    )
    terms = lax.all_to_all(terms.astype(jnp.bfloat16), "tp", split_axis=0, concat_axis=0, tiled=True)
    return jnp.sum(terms.astype(jnp.float32), axis=0).astype(jnp.bfloat16)


def solution(mesh):
    seq_size = mesh.shape["seq"]
    requests = 8
    grid = Mesh(
        np.asarray(mesh.devices).reshape(seq_size // requests, requests, mesh.shape["tp"]),
        ("place", "req", "tp"),
    )
    seq = ("place", "req")
    return jax.shard_map(
        layer,
        mesh=grid,
        in_specs=(
            P(seq, "tp"),
            P(seq, "tp"),
            P(seq, "tp"),
            P(None, seq, "tp"),
            P(None, seq, "tp"),
            P("tp", None),
            P(),
            P(),
            P(),
            P(),
        ),
        out_specs=P(seq, "tp"),
        check_vma=False,
    )
```

```python
import math

import jax
import jax.numpy as jnp
import numpy as np
from jax import lax
from jax.experimental import pallas as pl
from jax.experimental.pallas import tpu as pltpu
from jax.sharding import Mesh
from jax.sharding import PartitionSpec as P

HEAD = 128


NEG = -1e30


def attend(q_rows, chunks, span_k, span_v, params, places, interpret=False):
    total_rows, width = q_rows.shape
    rows = total_rows // places
    heads = width // HEAD
    n = len(chunks)
    cdev = chunks[0].shape[1]
    srows = span_k.shape[0]
    scale = 1.0 / math.sqrt(HEAD)

    def kernel(par, q_ref, *refs):
        kv_refs = refs[:n]
        sk_ref, sv_ref, o_ref, m_ref, l_ref = refs[n:]
        length = par[n + 1]
        window = par[n + 2]
        sinks = par[n + 3]
        row = lax.broadcasted_iota(jnp.int32, (total_rows, 1), 0)
        qpos = row % rows
        for j in range(places):
            qpos = jnp.where(row // rows == j, qpos + par[n + 4 + j], qpos)
        rows_here = total_rows
        q = q_ref[...]
        m = jnp.full((rows_here, 1), NEG, jnp.float32)
        l = jnp.zeros((rows_here, 1), jnp.float32)
        acc = jnp.zeros((rows_here, HEAD), jnp.float32)
        for c in range(n + 1):
            if c < n:
                keys = kv_refs[c][0]
                vals = kv_refs[c][1]
                kpos = par[c] + lax.broadcasted_iota(jnp.int32, (1, cdev), 1)
                valid = kpos < length
            else:
                keys = sk_ref[...]
                vals = sv_ref[...]
                kpos = par[n] + lax.broadcasted_iota(jnp.int32, (1, srows), 1)
                valid = kpos >= 0
            s = lax.dot_general(q, keys, (((1,), (1,)), ((), ())), preferred_element_type=jnp.float32) * scale
            mask = (kpos <= qpos) & ((qpos - kpos < window) | (kpos < sinks)) & valid
            s = jnp.where(mask, s, NEG)
            m_new = jnp.maximum(m, jnp.max(s, axis=1, keepdims=True))
            alpha = jnp.exp(m - m_new)
            p = jnp.exp(s - jnp.where(m_new > NEG, m_new, 0.0))
            l = alpha * l + jnp.sum(p, axis=1, keepdims=True)
            acc = alpha * acc + jnp.dot(p.astype(jnp.bfloat16), vals, preferred_element_type=jnp.float32)
            m = m_new
        o_ref[...] = acc.astype(o_ref.dtype)
        m_ref[...] = m
        l_ref[...] = l

    in_specs = [pl.BlockSpec((total_rows, HEAD), lambda h, par: (0, h))]
    in_specs += [pl.BlockSpec((2, cdev, HEAD), lambda h, par: (0, 0, h)) for _ in range(n)]
    in_specs += [pl.BlockSpec((srows, HEAD), lambda h, par: (0, h))] * 2
    out_specs = [
        pl.BlockSpec((total_rows, HEAD), lambda h, par: (0, h)),
        pl.BlockSpec((None, total_rows, 1), lambda h, par: (h, 0, 0)),
        pl.BlockSpec((None, total_rows, 1), lambda h, par: (h, 0, 0)),
    ]
    out_shape = [
        jax.ShapeDtypeStruct((total_rows, width), jnp.bfloat16),
        jax.ShapeDtypeStruct((heads, total_rows, 1), jnp.float32),
        jax.ShapeDtypeStruct((heads, total_rows, 1), jnp.float32),
    ]
    return pl.pallas_call(
        kernel,
        grid_spec=pltpu.PrefetchScalarGridSpec(
            num_scalar_prefetch=1, grid=(heads,), in_specs=in_specs, out_specs=out_specs
        ),
        out_shape=out_shape,
        interpret=interpret,
    )(params, q_rows, *chunks, span_k, span_v)


def layer(
    query,
    span_keys,
    span_values,
    cache_keys,
    cache_values,
    out_weight,
    cache_lengths,
    sink_counts,
    windows,
    block_of_slot,
):
    rows, width = query.shape
    heads_here = width // HEAD
    places = lax.axis_size("place")
    group = lax.axis_size("req")
    devices = places * group
    place = lax.axis_index("place")
    mine = lax.axis_index("req")
    me = place * group + mine
    cache_dev = cache_keys.shape[1]
    length = cache_lengths[mine]
    window = windows[mine]
    sinks = sink_counts[mine]
    seq = ("place", "req")

    ring = devices // 4
    core, z, y = me % 2, (me // 2) % ring, me // (2 * ring)

    def at(yy, zz, cc):
        return (yy * ring + zz % ring) * 2 + cc

    def request_of(index):
        return index % group

    moves = [(d, flip) for d in (-1, 0, 1) for flip in (0, 1)] + [("far", c) for c in (0, 1)]
    got_kv, got_slot = [], []
    for d, flip in moves:
        if d == "far":
            target = jnp.where(core == 0, at(y, z + 2, flip), at(y, z - 2, 1 - flip))
            source = jnp.where(core == flip, at(y, z - 2, 0), at(y, z + 2, 1))
            pairs = []
            for s_idx in range(devices):
                sc, sz, sy = s_idx % 2, (s_idx // 2) % ring, s_idx // (2 * ring)
                if sc == 0:
                    pairs.append((s_idx, (sy * ring + (sz + 2) % ring) * 2 + flip))
                else:
                    pairs.append((s_idx, (sy * ring + (sz - 2) % ring) * 2 + 1 - flip))
        else:
            target = at(y, z + d, core ^ flip)
            source = at(y, z - d, core ^ flip)
            pairs = []
            for s_idx in range(devices):
                sc, sz, sy = s_idx % 2, (s_idx // 2) % ring, s_idx // (2 * ring)
                pairs.append((s_idx, (sy * ring + (sz + d) % ring) * 2 + (sc ^ flip)))
        sent = request_of(target)
        chunk = jnp.stack(
            [
                lax.dynamic_index_in_dim(cache_keys, sent, 0, keepdims=False),
                lax.dynamic_index_in_dim(cache_values, sent, 0, keepdims=False),
            ]
        )
        if d != 0 or flip != 0:
            chunk = lax.ppermute(chunk, seq, pairs)
        got_kv.append(chunk)
        got_slot.append(source)

    span_q = [query]
    for k in range(1, places):
        pairs = [(p * group + i, ((p + k) % places) * group + i) for p in range(places) for i in range(group)]
        span_q.append(lax.ppermute(query, seq, pairs))
    span_q = jnp.stack(span_q)
    from_place = (place - jnp.arange(places, dtype=jnp.int32)) % places

    slots = jnp.stack(got_slot)
    blocks = block_of_slot[mine][slots]
    head_params = jnp.concatenate(
        [blocks * cache_dev, jnp.stack([length + place * rows, length, window, sinks])]
    )
    first_rows = length + from_place * rows

    def partial(picked):
        params = jnp.concatenate([head_params, first_rows[picked[0] : picked[-1] + 1]]).astype(jnp.int32)
        q_rows = span_q[picked[0] : picked[-1] + 1].reshape(-1, width)
        out, top, total = attend(q_rows, got_kv, span_keys, span_values, params, len(picked))
        stats = jnp.concatenate([top[..., 0].T, total[..., 0].T], axis=1)
        return out.reshape(len(picked), rows, width), stats.reshape(len(picked), rows, 2 * heads_here)

    other_sum, other_stats = partial(list(range(1, places)))
    own_sum, own_stats = partial([0])
    back_sum, back_stats = [own_sum[0]], [own_stats[0]]
    for k in range(1, places):
        pairs = [(p * group + i, ((p - k) % places) * group + i) for p in range(places) for i in range(group)]
        got = lax.ppermute((other_sum[k - 1], other_stats[k - 1]), seq, pairs)
        back_sum.append(got[0])
        back_stats.append(got[1])
    summed = jnp.stack(back_sum).astype(jnp.float32).reshape(places, rows, heads_here, HEAD)
    stats = jnp.stack(back_stats)
    top, total = stats[..., :heads_here], stats[..., heads_here:]
    best = jnp.max(top, axis=0)
    factor = jnp.exp(top - best[None])
    total = jnp.sum(total * factor, axis=0)
    summed = jnp.sum(summed * factor[..., None], axis=0)
    attention = (summed / total[..., None]).astype(jnp.bfloat16).reshape(rows, width)
    parts = lax.axis_size("tp")
    terms = jnp.einsum(
        "qf,fkc->kqc", attention, out_weight.reshape(width, parts, -1), preferred_element_type=jnp.float32
    )
    terms = terms.astype(jnp.bfloat16)
    me_tp = lax.axis_index("tp")
    result = lax.dynamic_index_in_dim(terms, me_tp, 0, keepdims=False).astype(jnp.float32)
    for shift in range(1, parts):
        sent = lax.dynamic_index_in_dim(terms, (me_tp + shift) % parts, 0, keepdims=False)
        got = lax.ppermute(sent, "tp", [(i, (i + shift) % parts) for i in range(parts)])
        result = result + got.astype(jnp.float32)
    return result.astype(jnp.bfloat16)


def solution(mesh):
    seq_size = mesh.shape["seq"]
    requests = 8
    grid = Mesh(
        np.asarray(mesh.devices).reshape(seq_size // requests, requests, mesh.shape["tp"]),
        ("place", "req", "tp"),
    )
    seq = ("place", "req")
    return jax.shard_map(
        layer,
        mesh=grid,
        in_specs=(
            P(seq, "tp"),
            P(seq, "tp"),
            P(seq, "tp"),
            P(None, seq, "tp"),
            P(None, seq, "tp"),
            P("tp", None),
            P(),
            P(),
            P(),
            P(),
        ),
        out_specs=P(seq, "tp"),
        check_vma=False,
    )
```
